32 devices in a mesh: dp: 2 (over y), tm: 4 (over z), label: 4 (over x, core).
Axes of the slice: x: 2, y: 2, z: 4, core: 2. Of those that a mesh axis runs over, the one named last changes fastest.
Arguments:
- encoder_out: bfloat16 [2, 512, 512], P('dp', 'tm', 'label'), may hold values from -8 to 8
- predictor_out: bfloat16 [2, 128, 512], P('dp', 'label', 'tm'), may hold values from -6 to 6
- label_ids: int32 [2, 128], P('dp', 'label'), may hold values from 1 to 511
- log_alpha: float32 [2, 512, 128], P('dp', 'tm', 'label'), may hold values from -2 to 0
- log_beta: float32 [2, 512, 128], P('dp', 'tm', 'label'), may hold values from -2 to 0
- frame_count: int32 [2], P('dp'), may hold values from 256 to 512, as said below
- label_count: int32 [2], P('dp'), may hold values from 32 to 127, as said below
- joint_weight: bfloat16 [512, 512], replicated, may hold values from -2 to 2
- joint_bias: float32 [512], replicated, may hold values from -5 to 10
Outputs:
- encoder_gradient: float32 [2, 512, 512], P('dp', 'tm', 'label')
- predictor_gradient: float32 [2, 128, 512], P('dp', 'label', 'tm')
- weight_gradient: float32 [512, 512], P(('tm', 'label'))
- bias_gradient: float32 [512], P(('tm', 'label'))
The draws below stay inside these ranges and needn't reach their ends.
Inputs may be any that keep to these rules, and one draw needn't show every extreme that they name: `frame_count`: some utterance has all 512 frames. `label_count`: some utterance has 127 labels.
All inputs are finite; a program needn't handle non-finite values.
Results may differ from the reference program's by a relative error of at most 0.0003.
The reference program's roundings to bfloat16 on the way (of `joint_act` and `logit_gradient`) count: a program that leaves them out, or rounds other values in their place, can miss the bound.
Values may be sent and summed in bfloat16 or wider, within the bound.
No kernel may reach another device: no remote copies, remote signals or barrier semaphores. Data moves between devices by JAX's collectives and lax.ppermute only.
A program may use at most 64 MiB of HBM per device.

```python
import math
import jax
import jax.numpy as jnp
from jax import lax

H = 512
V = 512
BATCH = 2
FRAMES = 512
COLS = 128


def draw_encoder_out(key, part):
    base = jnp.clip(jax.random.normal(key, (BATCH, FRAMES, H), jnp.float32), -6.0, 6.0)
    return base.astype(jnp.bfloat16)


def draw_joint_weight(key, part):
    spread = 4.0 / math.sqrt(H)
    base = jnp.clip(jax.random.normal(key, (H, V), jnp.float32), -5.0, 5.0) * spread
    return base.astype(jnp.bfloat16)


def draw_joint_bias(key, part):
    blank_key = jax.random.fold_in(key, 31)
    base = jnp.clip(jax.random.normal(key, (V,), jnp.float32), -5.0, 5.0)
    blank_value = jax.random.uniform(blank_key, (), jnp.float32, 8.0, 10.0)
    return jnp.where(jnp.arange(V) == 0, blank_value, base).astype(jnp.float32)


def draw_frame_count(key, part):
    first_key, second_key = jax.random.split(jax.random.fold_in(key, 21))
    drawn = jax.random.randint(first_key, (BATCH,), FRAMES // 2, FRAMES + 1)
    full_one = jax.random.randint(second_key, (), 0, BATCH)
    return jnp.where(jnp.arange(BATCH) == full_one, FRAMES, drawn).astype(jnp.int32)


def draw_label_count(key, part):
    first_key, second_key = jax.random.split(jax.random.fold_in(key, 22))
    drawn = jax.random.randint(first_key, (BATCH,), COLS // 4, COLS)
    full_one = jax.random.randint(second_key, (), 0, BATCH)
    return jnp.where(jnp.arange(BATCH) == full_one, COLS - 1, drawn).astype(jnp.int32)


def set_ends(result, key, least, largest):
    index_at = [jax.random.randint(jax.random.fold_in(key, axis), (), 0, length) for axis, length in enumerate(result.shape)]
    widest = result.shape.index(max(result.shape))
    neighbour = index_at[:widest] + [(index_at[widest] + 1) % result.shape[widest]] + index_at[widest + 1:]
    return result.at[tuple(index_at)].set(least).at[tuple(neighbour)].set(largest)


def block_scale(own_key, extent, pieces, least, top_value):
    factor_of, own = 1.0, jax.random.fold_in(own_key, 6)
    for position, parts in pieces:
        steps = jnp.exp(jax.random.uniform(jax.random.fold_in(own, position), (parts,), jnp.float32, least / len(pieces), top_value / len(pieces)))
        factor_of = factor_of * jnp.repeat(steps, extent[position] // parts).reshape([-1 if axis == position else 1 for axis in range(len(extent))])
    return factor_of


def centred(own_key, dims, width, reach, shards=(), kind=jnp.bfloat16):
    result = width * jax.random.normal(own_key, dims, jnp.float32)
    if shards:
        result = result * block_scale(own_key, dims, shards, -0.22, 0.18)
    return jnp.clip(result, -reach, reach).astype(kind)


def setup_inputs(seed: int = 0) -> dict:
    streams_of = jax.random.split(jax.random.key(seed), 10)
    encoder_out = draw_encoder_out(jax.random.fold_in(streams_of[9], 71), 0)
    predictor_out = centred(streams_of[1], (BATCH, COLS, H), 1.0, 6.0, ((0, 2), (1, 4), (2, 4)))
    label_ids = set_ends(jax.random.randint(streams_of[2], (BATCH, COLS), 1, V), jax.random.fold_in(streams_of[2], 1), 1, V - 1).astype(jnp.int32)
    log_alpha = jnp.clip(-2.0 + 2.0 * jax.random.uniform(streams_of[3], (BATCH, FRAMES, COLS), jnp.float32) ** block_scale(streams_of[3], (BATCH, FRAMES, COLS), ((0, 2), (1, 4), (2, 4)), -0.2, 0.2), -2.0, 0.0)
    log_beta = jnp.clip(-2.0 + 2.0 * jax.random.uniform(streams_of[4], (BATCH, FRAMES, COLS), jnp.float32) ** block_scale(streams_of[4], (BATCH, FRAMES, COLS), ((0, 2), (1, 4), (2, 4)), -0.2, 0.2), -2.0, 0.0)
    frame_count = draw_frame_count(jax.random.fold_in(streams_of[9], 71), 0)
    label_count = draw_label_count(jax.random.fold_in(streams_of[9], 71), 0)
    joint_weight = draw_joint_weight(jax.random.fold_in(streams_of[9], 71), 0)
    joint_bias = draw_joint_bias(jax.random.fold_in(streams_of[9], 71), 0)
    return {"encoder_out": encoder_out, "predictor_out": predictor_out, "label_ids": label_ids, "log_alpha": log_alpha, "log_beta": log_beta, "frame_count": frame_count, "label_count": label_count, "joint_weight": joint_weight, "joint_bias": joint_bias}


def lattice(frame_rows, label_rows, label_row, alpha_rows, beta_rows, beta_down, beta_right, row_start, col_start, frame_limit, label_limit, score, weight_matrix, bias_vector):
    row_count, joint_width = frame_rows.shape
    col_count = label_rows.shape[0]
    vocab_size = weight_matrix.shape[1]
    summed = frame_rows.astype(jnp.float32)[:, None, :] + label_rows.astype(jnp.float32)[None, :, :]
    joint_act = jnp.tanh(summed).astype(jnp.bfloat16).reshape(row_count * col_count, joint_width)
    logits = jnp.dot(joint_act, weight_matrix, preferred_element_type=jnp.float32) + bias_vector[None, :]
    peak_value = jnp.max(logits, axis=1, keepdims=True)
    log_total = peak_value + jnp.log(jnp.sum(jnp.exp(logits - peak_value), axis=1, keepdims=True))
    probability = jnp.exp(logits - log_total)
    symbol = lax.broadcasted_iota(jnp.int32, (1, vocab_size), 1)
    label_cells = jnp.broadcast_to(label_row[None, :], (row_count, col_count)).reshape(row_count * col_count, 1)
    chosen = symbol == label_cells
    blank_score = (logits[:, 0] - log_total[:, 0]).reshape(row_count, col_count)
    label_score = (jnp.sum(jnp.where(chosen, logits, 0.0), axis=1) - log_total[:, 0]).reshape(row_count, col_count)
    frame_pos = row_start + jnp.arange(row_count, dtype=jnp.int32)[:, None]
    col_pos = col_start + jnp.arange(col_count, dtype=jnp.int32)[None, :]
    inside = (frame_pos < frame_limit) & (col_pos <= label_limit)
    blank_live = inside & ((frame_pos + 1 < frame_limit) | (col_pos == label_limit))
    label_live = inside & (col_pos < label_limit)
    after_blank = jnp.where(frame_pos + 1 < frame_limit, beta_down, 0.0)
    occupancy = jnp.where(inside, jnp.exp(alpha_rows + beta_rows - score), 0.0).reshape(-1, 1)
    blank_weight = jnp.where(blank_live, jnp.exp(alpha_rows + blank_score + after_blank - score), 0.0).reshape(-1, 1)
    label_weight = jnp.where(label_live, jnp.exp(alpha_rows + label_score + beta_right - score), 0.0).reshape(-1, 1)
    logit_gradient = (occupancy * probability - jnp.where(symbol == 0, blank_weight, 0.0) - jnp.where(chosen, label_weight, 0.0)).astype(jnp.bfloat16)
    back_gradient = lax.dot_general(logit_gradient, weight_matrix, (((1,), (1,)), ((), ())), preferred_element_type=jnp.float32)
    joint_wide = joint_act.astype(jnp.float32)
    cell_gradient = (back_gradient * (1.0 - joint_wide * joint_wide)).reshape(row_count, col_count, joint_width)
    weight_term = lax.dot_general(joint_act, logit_gradient, (((0,), (0,)), ((), ())), preferred_element_type=jnp.float32)
    return cell_gradient.sum(axis=1), cell_gradient.sum(axis=0), weight_term, logit_gradient.astype(jnp.float32).sum(axis=0)


def reference(encoder_out, predictor_out, label_ids, log_alpha, log_beta, frame_count, label_count, joint_weight, joint_bias):
    block_rows = 16
    block_count = FRAMES // block_rows
    joint_width = joint_weight.shape[0]
    vocab_size = joint_weight.shape[1]
    weight_sum = jnp.zeros((joint_width, vocab_size), jnp.float32)
    bias_sum = jnp.zeros((vocab_size,), jnp.float32)
    frame_parts = []
    label_parts = []
    for utterance in range(BATCH):
        beta_slab = log_beta[utterance]
        beta_down = jnp.concatenate([beta_slab[1:], jnp.zeros((1, COLS), jnp.float32)], axis=0)
        beta_right = jnp.concatenate([beta_slab[:, 1:], jnp.zeros((FRAMES, 1), jnp.float32)], axis=1)
        score = beta_slab[0, 0]

        def advance(running, block_idx, utterance=utterance, beta_down=beta_down, beta_right=beta_right, score=score):
            first_row = block_idx * block_rows

            def take_rows(source):
                return lax.dynamic_slice_in_dim(source, first_row, block_rows, 0)

            frame_term, label_term, weight_term, bias_term = lattice(
                take_rows(encoder_out[utterance]), predictor_out[utterance], label_ids[utterance],
                take_rows(log_alpha[utterance]), take_rows(log_beta[utterance]), take_rows(beta_down), take_rows(beta_right),
                first_row, jnp.int32(0), frame_count[utterance], label_count[utterance], score, joint_weight, joint_bias)
            return (running[0] + label_term, running[1] + weight_term, running[2] + bias_term), frame_term

        start_state = (jnp.zeros((COLS, joint_width), jnp.float32), weight_sum, bias_sum)
        (label_sum, weight_sum, bias_sum), frame_blocks = lax.scan(advance, start_state, jnp.arange(block_count, dtype=jnp.int32))
        frame_parts.append(frame_blocks.reshape(FRAMES, joint_width))
        label_parts.append(label_sum)
    return (jnp.stack(frame_parts), jnp.stack(label_parts), weight_sum, bias_sum)
```

```python
import functools

import jax
import jax.numpy as jnp
from jax import lax
from jax.experimental import pallas as pl
from jax.experimental.pallas import tpu as pltpu
from jax.sharding import PartitionSpec as P

GROUP = 4
CHUNK = 16
LANES = 128
FAR = -1e30


def bits_of(size):
    return [1 << i for i in range(size.bit_length() - 1)]


def reverse_bits(value, size):
    width = size.bit_length() - 1
    result = 0
    for i in range(width):
        result = result | (((value >> i) & 1) << (width - 1 - i))
    return result


def swap(value, axis, bit):
    return lax.ppermute(value, axis, [(i, i ^ bit) for i in range(lax.axis_size(axis))])


def gather_slots(value, axis):
    slots = value[None]
    for bit in bits_of(lax.axis_size(axis)):
        slots = jnp.concatenate([slots, swap(slots, axis, bit)], axis=0)
    return slots


def scatter_slots(slots, axis):
    for bit in bits_of(lax.axis_size(axis)):
        half = slots.shape[0] // 2
        slots = slots[:half] + swap(slots[half:], axis, bit)
    return slots[0]


def forward_kernel(
    ids_ref,
    frames_ref,
    labels_ref,
    enc_ref,
    pred_ref,
    side_ref,
    alpha_ref,
    beta_ref,
    wt_ref,
    bias_ref,
    act_ref,
    grad_ref,
    *rest,
    tm_size,
    label_size,
):
    out_refs, (enc_t, pred_t, bias_t, occ_s, blank_s, label_s, lt, acc) = rest[:-8], rest[-8:]
    step = pl.program_id(0)
    columns, frames = alpha_ref.shape
    width, vocab = wt_ref.shape[1], wt_ref.shape[0]
    mine, row = lax.axis_index("label"), lax.axis_index("tm")

    @pl.when(step == 0)
    def _():
        enc_width = enc_ref.shape[2]
        for s in range(label_size):
            start = pl.multiple_of((mine ^ s) * enc_width, enc_width)
            enc_t[pl.ds(start, enc_width), :] = enc_ref[s].astype(jnp.float32).T
        pred_width = pred_ref.shape[2]
        pred_t[...] = jnp.zeros_like(pred_t)
        for s in range(tm_size):
            start = pl.multiple_of((row ^ s) * pred_width, pred_width)
            pred_t[pl.ds(start, pred_width), :columns] = pred_ref[s, :columns, :].T
        bias_t[...] = jnp.broadcast_to(bias_ref[...], (frames, vocab)).T
        acc[...] = jnp.zeros_like(acc)
        alpha, beta = alpha_ref[...], beta_ref[...]
        score = pred_ref[row, columns + 1 : columns + 2, 0:1]
        below = pred_ref[row ^ jnp.minimum(row + 1, tm_size - 1), columns : columns + 1, :columns]
        beside = side_ref[mine ^ jnp.minimum(mine + 1, label_size - 1)]
        lane = lax.broadcasted_iota(jnp.int32, (columns, frames), 1)
        line = lax.broadcasted_iota(jnp.int32, (columns, frames), 0)
        below = jnp.broadcast_to(below, (columns, columns))
        below = jnp.sum(
            jnp.where(
                lax.broadcasted_iota(jnp.int32, (columns, columns), 0)
                == lax.broadcasted_iota(jnp.int32, (columns, columns), 1),
                below,
                0.0,
            ),
            axis=1,
            keepdims=True,
        )
        down = jnp.where(lane == frames - 1, below, pltpu.roll(beta, frames - 1, 1))
        right = jnp.where(line == columns - 1, beside, pltpu.roll(beta, columns - 1, 0))
        frame = row * frames + lane
        column = mine * columns + line
        frame_limit, label_limit = frames_ref[0], labels_ref[0]
        inside = (frame < frame_limit) & (column <= label_limit)
        more = frame + 1 < frame_limit
        occ_s[...] = jnp.where(inside, jnp.exp(alpha + beta - score), 0.0)
        blank_s[...] = jnp.where(
            inside & (more | (column == label_limit)),
            alpha + jnp.where(more, down, 0.0) - score,
            FAR,
        )
        label_s[...] = jnp.where(inside & (column < label_limit), alpha + right - score, FAR)

    shift = lax.rem(LANES - step * GROUP, LANES)
    turned = pltpu.roll(pred_t[...], shift, 1)
    for j in range(GROUP):
        here = slice(j * frames, (j + 1) * frames)
        for c in range(0, width, 64):
            total = enc_t[c : c + 64, :] + turned[c : c + 64, j : j + 1]
            act_ref[c : c + 64, here] = jnp.tanh(total).astype(jnp.bfloat16)
    act_ref[width:, :] = jnp.ones((act_ref.shape[0] - width, GROUP * frames), jnp.bfloat16)
    product = jnp.dot(wt_ref[...], act_ref[:width, :], preferred_element_type=jnp.float32)
    for j in range(GROUP):
        lt[j] = product[:, j * frames : (j + 1) * frames]

    peak = jnp.full((GROUP, 8, frames), FAR, jnp.float32)
    for c in range(0, vocab, CHUNK):
        logits = lt[:, c : c + CHUNK, :] + bias_t[c : c + CHUNK, :][None]
        lt[:, c : c + CHUNK, :] = logits
        for k in range(0, CHUNK, 8):
            peak = jnp.maximum(peak, logits[:, k : k + 8, :])
    peak = jnp.max(peak, axis=1, keepdims=True)

    ids = [ids_ref[0, step * GROUP + j] for j in range(GROUP)]
    blank_logit = lt[:, 0:1, :]
    label_logit = jnp.concatenate([lt[j, pl.ds(ids[j], 1), :][None] for j in range(GROUP)], axis=0)

    def line_of(ref):
        return jnp.concatenate(
            [ref[pl.ds(step * GROUP + j, 1), :][None] for j in range(GROUP)], axis=0
        )

    total = jnp.zeros((GROUP, 8, frames), jnp.float32)
    for c in range(0, vocab, CHUNK):
        lifted = jnp.exp(lt[:, c : c + CHUNK, :] - peak)
        lt[:, c : c + CHUNK, :] = lifted
        for k in range(0, CHUNK, 8):
            total = total + lifted[:, k : k + 8, :]
    total = jnp.sum(total, axis=1, keepdims=True)
    log_total = peak + jnp.log(total)
    scale = line_of(occ_s) / total
    blank_weight = jnp.exp(line_of(blank_s) + (blank_logit - log_total))
    label_weight = jnp.exp(line_of(label_s) + (label_logit - log_total))

    place = lax.broadcasted_iota(jnp.int32, (CHUNK, frames), 0)
    for j in range(GROUP):
        here = slice(j * frames, (j + 1) * frames)
        for c in range(0, vocab, CHUNK):
            grad_ref[c : c + CHUNK, here] = (lt[j, c : c + CHUNK, :] * scale[j]).astype(jnp.bfloat16)
        for first in (0, pl.multiple_of((ids[j] // CHUNK) * CHUNK, CHUNK)):
            value = lt[j, pl.ds(first, CHUNK), :] * scale[j]
            value = value - jnp.where(place + first == 0, blank_weight[j], 0.0)
            value = value - jnp.where(place + first == ids[j], label_weight[j], 0.0)
            grad_ref[pl.ds(first, CHUNK), here] = value.astype(jnp.bfloat16)

    acc[...] += lax.dot_general(
        act_ref[...], grad_ref[...], (((1,), (1,)), ((), ())), preferred_element_type=jnp.float32
    )

    @pl.when(step == pl.num_programs(0) - 1)
    def _():
        if len(out_refs) == 1:
            out_refs[0][...] = acc[: width + 8, :]
            return
        parts = tm_size * label_size
        rows = width // parts
        for s in range(parts):
            label = reverse_bits(s // tm_size, label_size) ^ mine
            tm = reverse_bits(s % tm_size, tm_size) ^ row
            start = pl.multiple_of((tm * label_size + label) * rows, rows)
            ref = out_refs[s // (parts // 2)]
            to = (s % (parts // 2)) * rows
            ref[to : to + rows, :] = acc[pl.ds(start, rows), :]
        for ref in out_refs:
            ref[width // 2 :, :] = acc[width : width + 8, :]


def backward_kernel(
    act_ref, grad_ref, w_ref, enc_out, pred_out, bt, enc_acc, pred_acc, *, tm_size, label_size, columns
):
    step = pl.program_id(0)
    width = w_ref.shape[0]
    frames = enc_acc.shape[1]

    @pl.when(step == 0)
    def _():
        enc_acc[...] = jnp.zeros_like(enc_acc)
        pred_acc[...] = jnp.zeros_like(pred_acc)

    bt[...] = jnp.dot(w_ref[...], grad_ref[...], preferred_element_type=jnp.float32)
    lane = lax.broadcasted_iota(jnp.int32, (CHUNK, LANES), 1)
    for c in range(0, width, CHUNK):
        act = act_ref[c : c + CHUNK, :].astype(jnp.float32)
        cell = bt[c : c + CHUNK, :] * (1.0 - act * act)
        total = enc_acc[c : c + CHUNK, :]
        kept = pred_acc[c : c + CHUNK, :]
        for j in range(GROUP):
            part = cell[:, j * frames : (j + 1) * frames]
            total = total + part
            kept = jnp.where(lane == step * GROUP + j, jnp.sum(part, axis=1, keepdims=True), kept)
        enc_acc[c : c + CHUNK, :] = total
        pred_acc[c : c + CHUNK, :] = kept

    @pl.when(step == pl.num_programs(0) - 1)
    def _():
        mine, row = lax.axis_index("label"), lax.axis_index("tm")
        enc_width, pred_width = enc_out.shape[2], pred_out.shape[2]
        for s in range(label_size):
            start = pl.multiple_of((reverse_bits(s, label_size) ^ mine) * enc_width, enc_width)
            enc_out[s] = enc_acc[pl.ds(start, enc_width), :].T
        for s in range(tm_size):
            start = pl.multiple_of((reverse_bits(s, tm_size) ^ row) * pred_width, pred_width)
            pred_out[s] = pred_acc[pl.ds(start, pred_width), :].T[:columns, :]


def whole(shape):
    return pl.BlockSpec(shape, lambda i, *_: (0,) * len(shape))


def run_forward(
    ids, frame_count, label_count, enc, pred, side, alpha, beta, weight_t, bias, split, tm_size, label_size
):
    columns, frames = alpha.shape
    vocab, width = weight_t.shape
    cells = GROUP * frames
    operands = (enc, pred, side, alpha, beta, weight_t, bias)
    out_shape = [
        jax.ShapeDtypeStruct((width + 16, columns * frames), jnp.bfloat16),
        jax.ShapeDtypeStruct((vocab, columns * frames), jnp.bfloat16),
    ]
    out_specs = [
        pl.BlockSpec((width + 16, cells), lambda i, *_: (0, i)),
        pl.BlockSpec((vocab, cells), lambda i, *_: (0, i)),
    ]
    count, rows = (2, width // 2 + 8) if split else (1, width + 8)
    for _ in range(count):
        out_shape.append(jax.ShapeDtypeStruct((rows, vocab), jnp.float32))
        out_specs.append(whole((rows, vocab)))
    return pl.pallas_call(
        functools.partial(forward_kernel, tm_size=tm_size, label_size=label_size),
        grid_spec=pltpu.PrefetchScalarGridSpec(
            num_scalar_prefetch=3,
            grid=(columns // GROUP,),
            in_specs=[whole(x.shape) for x in operands],
            out_specs=out_specs,
            scratch_shapes=[
                pltpu.VMEM((width, frames), jnp.float32),
                pltpu.VMEM((width, LANES), jnp.float32),
                pltpu.VMEM((vocab, frames), jnp.float32),
                pltpu.VMEM((columns, frames), jnp.float32),
                pltpu.VMEM((columns, frames), jnp.float32),
                pltpu.VMEM((columns, frames), jnp.float32),
                pltpu.VMEM((GROUP, vocab, frames), jnp.float32),
                pltpu.VMEM((width + 16, vocab), jnp.float32),
            ],
        ),
        out_shape=out_shape,
        name="forward",
    )(ids, frame_count, label_count, *operands)


def run_backward(act, grad, weight, frames, columns, tm_size, label_size):
    width, vocab = weight.shape
    cells = GROUP * frames
    enc_shape = (label_size, frames, width // label_size)
    pred_shape = (tm_size, columns, width // tm_size)
    return pl.pallas_call(
        functools.partial(
            backward_kernel, tm_size=tm_size, label_size=label_size, columns=columns
        ),
        grid=(columns // GROUP,),
        in_specs=[
            pl.BlockSpec((width, cells), lambda i: (0, i)),
            pl.BlockSpec((vocab, cells), lambda i: (0, i)),
            whole((width, vocab)),
        ],
        out_specs=[whole(enc_shape), whole(pred_shape)],
        scratch_shapes=[
            pltpu.VMEM((width, cells), jnp.float32),
            pltpu.VMEM((width, frames), jnp.float32),
            pltpu.VMEM((width, LANES), jnp.float32),
        ],
        out_shape=[
            jax.ShapeDtypeStruct(enc_shape, jnp.float32),
            jax.ShapeDtypeStruct(pred_shape, jnp.float32),
        ],
        name="backward",
    )(act, grad, weight)


def per_device(
    encoder_out,
    predictor_out,
    label_ids,
    log_alpha,
    log_beta,
    frame_count,
    label_count,
    joint_weight,
    joint_bias,
):
    frames, columns = encoder_out.shape[1], label_ids.shape[1]
    width, vocab = joint_weight.shape
    tm_size, label_size = lax.axis_size("tm"), lax.axis_size("label")
    parts = tm_size * label_size
    rows = width // parts
    row, mine = lax.axis_index("tm"), lax.axis_index("label")
    alpha, beta = log_alpha[0].T, log_beta[0].T

    side = gather_slots(beta[0:1, :], "label")
    enc = gather_slots(encoder_out[0], "label")
    pred_width = predictor_out.shape[2]
    first_score = side[mine, 0, 0]
    extra = jnp.concatenate(
        [
            jnp.pad(beta[:, 0][None, :], ((0, 0), (0, pred_width - columns))),
            jnp.broadcast_to(first_score, (7, pred_width)),
        ],
        axis=0,
    )
    pred = gather_slots(
        jnp.concatenate([predictor_out[0].astype(jnp.float32), extra], axis=0), "tm"
    )
    split = rows % 8 == 0
    act, grad, *weight_parts = run_forward(
        label_ids,
        frame_count,
        label_count,
        enc,
        pred,
        side,
        alpha,
        beta,
        joint_weight.T,
        joint_bias[None, :],
        split,
        tm_size,
        label_size,
    )
    if split:
        keep, send = weight_parts
        keep, bias_sum = keep[: width // 2], keep[width // 2 :]
    else:
        total, bias_sum = weight_parts[0][:width], weight_parts[0][width:]
        slots = total.reshape(tm_size, label_size, rows, vocab)
        for axis, size, index in ((0, tm_size, row), (1, label_size, mine)):
            order = jnp.array([reverse_bits(s, size) for s in range(size)], jnp.int32) ^ index
            slots = jnp.take(slots, order, axis=axis)
        slots = jnp.swapaxes(slots, 0, 1).reshape(width, vocab)
        keep, send = slots[: width // 2], slots[width // 2 :]
        send = jnp.concatenate([send, bias_sum], axis=0)

    stages = [("label", bit) for bit in bits_of(label_size)] + [("tm", bit) for bit in bits_of(tm_size)]
    first = swap(send, *stages[0])
    enc_slots, pred_slots = run_backward(
        act, grad, joint_weight, frames, columns, tm_size, label_size
    )
    arrived = first
    for i, _ in enumerate(stages):
        count = keep.shape[0]
        keep, bias_sum = keep + arrived[:count], bias_sum + arrived[count:]
        if i + 1 < len(stages):
            half = count // 2
            send = jnp.concatenate([keep[half:], bias_sum], axis=0)
            keep = keep[:half]
            arrived = swap(send, *stages[i + 1])
    final = jnp.concatenate([keep, bias_sum], axis=0)
    for bit in bits_of(lax.axis_size("dp")):
        final = final + swap(final, "dp", bit)
    weight_gradient = final[:rows]
    bias_rows = vocab // parts
    position = row * label_size + mine
    bias_gradient = lax.dynamic_slice_in_dim(final[rows], position * bias_rows, bias_rows, 0)

    encoder_gradient = scatter_slots(enc_slots, "label")[None]
    predictor_gradient = scatter_slots(pred_slots, "tm")[None]
    return (encoder_gradient, predictor_gradient, weight_gradient, bias_gradient)


def solution(mesh):
    return jax.shard_map(
        per_device,
        mesh=mesh,
        in_specs=(
            P("dp", "tm", "label"),
            P("dp", "label", "tm"),
            P("dp", "label"),
            P("dp", "tm", "label"),
            P("dp", "tm", "label"),
            P("dp"),
            P("dp"),
            P(),
            P(),
        ),
        out_specs=(
            P("dp", "tm", "label"),
            P("dp", "label", "tm"),
            P(("tm", "label"), None),
            P(("tm", "label")),
        ),
        check_vma=False,
    )
```

```python
import functools

import jax
import jax.numpy as jnp
from jax import lax
from jax.experimental import pallas as pl
from jax.experimental.pallas import tpu as pltpu
from jax.sharding import PartitionSpec as P

GROUP = 4
CHUNK = 16
LANES = 128
FAR = -1e30
MIB = 1 << 20


def bits_of(size):
    return [1 << i for i in range(size.bit_length() - 1)]


def reverse_bits(value, size):
    width = size.bit_length() - 1
    result = 0
    for i in range(width):
        result = result | (((value >> i) & 1) << (width - 1 - i))
    return result


def swap(value, axis, bit):
    return lax.ppermute(value, axis, [(i, i ^ bit) for i in range(lax.axis_size(axis))])


def gather_slots(value, axis):
    return [value] + [swap(value, axis, s) for s in range(1, lax.axis_size(axis))]


def vmem():
    return pl.BlockSpec(memory_space=pltpu.VMEM)


def loaded(kernel, loads, outputs):
    def body(*refs):
        sources, others, outs = refs[:loads], refs[loads:-loads - 1 - outputs], refs[-loads - 1 - outputs : -loads - 1]
        targets, done = refs[-loads - 1 : -1], refs[-1]
        copies = [
            pltpu.make_async_copy(source, target, done.at[i])
            for i, (source, target) in enumerate(zip(sources, targets))
        ]
        for copy in copies:
            copy.start()
        for copy in copies:
            copy.wait()
        kernel(*targets, *others, *outs)

    return body


def call(kernel, out_shape, operands, scratch=(), scalars=0, loads=0, limit=16, flops=0):
    resident = len(operands) - scalars - loads
    scratch = list(scratch)
    operands = list(operands)
    for i in range(scalars, scalars + loads):
        operands[i] = pltpu.with_memory_space_constraint(operands[i], pltpu.HBM)
    if loads:
        kernel = loaded(kernel, loads, len(out_shape))
        scratch += [pltpu.VMEM(x.shape, x.dtype) for x in operands[scalars : scalars + loads]]
        scratch.append(pltpu.SemaphoreType.DMA((loads,)))
    return pl.pallas_call(
        kernel,
        grid_spec=pltpu.PrefetchScalarGridSpec(
            num_scalar_prefetch=scalars,
            grid=(1,),
            in_specs=[pl.BlockSpec(memory_space=pltpu.HBM)] * loads + [vmem()] * resident,
            out_specs=[vmem()] * len(out_shape),
            scratch_shapes=scratch,
        ),
        out_shape=out_shape,
        compiler_params=pltpu.CompilerParams(vmem_limit_bytes=limit * MIB),
        cost_estimate=pl.CostEstimate(flops=flops, bytes_accessed=0, transcendentals=0) if flops else None,
    )(*operands)


def pack_encoder(enc_ref, beta_ref, out_ref):
    frames = enc_ref.shape[0]
    first = beta_ref[0:1, :]
    high = first.astype(jnp.bfloat16).astype(jnp.float32)
    middle = (first - high).astype(jnp.bfloat16).astype(jnp.float32)
    low = first - high - middle
    pieces = jnp.concatenate([high, middle, low, jnp.zeros((13, frames), jnp.float32)], axis=0)
    out_ref[:frames, :] = enc_ref[...]
    out_ref[frames:, :] = pieces.astype(jnp.bfloat16)


def side_line(ref, packed):
    if not packed:
        return ref[0:1, :]
    pieces = ref[ref.shape[0] - 16 :, :].astype(jnp.float32)
    return pieces[0:1, :] + pieces[1:2, :] + pieces[2:3, :]


def pick(refs, index, packed):
    return sum(jnp.where(index == s, side_line(ref, packed), 0.0) for s, ref in enumerate(refs))


def prepare(
    pred_ref, beta_ref, alpha_ref, w_ref, bias_ref, ids_ref, pred_out, alpha_out, beta_out, w_out, wt_out, bias_t, ids_out
):
    ids_out[...] = ids_ref[...]
    columns = pred_ref.shape[0]
    pred_out[:columns, :] = pred_ref[...].astype(jnp.float32)
    pred_out[columns:, :] = jnp.zeros((8, pred_out.shape[1]), jnp.float32)
    pred_out[columns : columns + 1, :columns] = beta_ref[...].T[0:1, :]
    alpha_out[...] = alpha_ref[...]
    beta_out[...] = beta_ref[...]
    w_out[...] = w_ref[...]
    wt_out[...] = w_ref[...].T
    bias_t[...] = jnp.broadcast_to(bias_ref[...], (bias_t.shape[1], bias_t.shape[0])).T


def pack_predictor(pred_ref, *rest, packed):
    side_refs, out_ref = rest[:-1], rest[-1]
    columns = pred_ref.shape[0] - 8
    out_ref[...] = pred_ref[...]
    score = pick(side_refs, lax.axis_index("label"), packed)[0:1, 0:1]
    out_ref[columns + 1 : columns + 2, :] = jnp.broadcast_to(score, (1, out_ref.shape[1]))


def forward_kernel(*refs, tm_size, label_size, packed, split):
    refs = iter(refs)
    take = lambda count: [next(refs) for _ in range(count)]
    ids_ref, frames_ref, labels_ref, alpha_ref, beta_ref, wt_ref, bias_t = take(7)
    enc_refs, pred_refs = take(label_size), take(tm_size)
    side_refs = enc_refs if packed else take(label_size)
    act_ref, grad_ref = take(2)
    out_refs = take(2 if split else 1)
    enc_t, pred_t, occ_s, blank_s, label_s, acc = take(6)
    lts = list(refs)
    columns, frames = alpha_ref.shape
    vocab, width = wt_ref.shape
    mine, row = lax.axis_index("label"), lax.axis_index("tm")

    enc_width, pred_width = enc_refs[0].shape[1], pred_refs[0].shape[1]
    for s, ref in enumerate(enc_refs):
        start = pl.multiple_of((mine ^ s) * enc_width, enc_width)
        enc_t[pl.ds(start, enc_width), :] = ref[:frames, :].astype(jnp.float32).T
    for s, ref in enumerate(pred_refs):
        start = pl.multiple_of((row ^ s) * pred_width, pred_width)
        pred_t[pl.ds(start, pred_width), :columns] = ref[:columns, :].T

    alpha, beta = alpha_ref[...], beta_ref[...]
    score, below = 0.0, 0.0
    after = row ^ jnp.minimum(row + 1, tm_size - 1)
    for s, ref in enumerate(pred_refs):
        score = score + jnp.where(row == s, ref[columns + 1 : columns + 2, 0:1], 0.0)
        below = below + jnp.where(after == s, ref[columns : columns + 1, :columns], 0.0)
    beside = pick(side_refs, mine ^ jnp.minimum(mine + 1, label_size - 1), packed)
    diagonal = lax.broadcasted_iota(jnp.int32, (columns, columns), 0) == lax.broadcasted_iota(
        jnp.int32, (columns, columns), 1
    )
    below = jnp.sum(jnp.where(diagonal, below, 0.0), axis=1, keepdims=True)
    lane = lax.broadcasted_iota(jnp.int32, (columns, frames), 1)
    line = lax.broadcasted_iota(jnp.int32, (columns, frames), 0)
    down = jnp.where(lane == frames - 1, below, pltpu.roll(beta, frames - 1, 1))
    right = jnp.where(line == columns - 1, beside, pltpu.roll(beta, columns - 1, 0))
    frame, column = row * frames + lane, mine * columns + line
    frame_limit, label_limit = frames_ref[0], labels_ref[0]
    inside = (frame < frame_limit) & (column <= label_limit)
    more = frame + 1 < frame_limit
    occ_s[...] = jnp.where(inside, jnp.exp(alpha + beta - score), 0.0)
    blank_s[...] = jnp.where(
        inside & (more | (column == label_limit)),
        alpha + jnp.where(more, down, 0.0) - score,
        FAR,
    )
    label_s[...] = jnp.where(inside & (column < label_limit), alpha + right - score, FAR)

    act_ref[width:, :] = jnp.ones((act_ref.shape[0] - width, columns * frames), jnp.bfloat16)
    groups = columns // GROUP
    cells = GROUP * frames
    peaks = {}

    def column_of(g, j):
        return reverse_bits(g, groups) + groups * j

    def activate(g):
        for j in range(GROUP):
            u, at = column_of(g, j), (g * GROUP + j) * frames
            for c in range(0, width, 64):
                total = enc_t[c : c + 64, :] + pred_t[c : c + 64, u : u + 1]
                act_ref[c : c + 64, at : at + frames] = jnp.tanh(total).astype(jnp.bfloat16)

    def score_logits(g):
        product = jnp.dot(
            wt_ref[...],
            act_ref[:width, g * cells : (g + 1) * cells],
            preferred_element_type=jnp.float32,
        )
        for j in range(GROUP):
            lt = lts[(g % 2) * GROUP + j]
            logits = product[:, j * frames : (j + 1) * frames] + bias_t[...]
            lt[...] = logits
            peaks[g, j] = jnp.max(logits, axis=0, keepdims=True)

    place = lax.broadcasted_iota(jnp.int32, (CHUNK, frames), 0)

    def differentiate(g):
        for j in range(GROUP):
            u, at = column_of(g, j), (g * GROUP + j) * frames
            lt, peak = lts[(g % 2) * GROUP + j], peaks[g, j]
            here = slice(at, at + frames)
            label = ids_ref[0, u]
            blank_logit, label_logit = lt[0:1, :], lt[pl.ds(label, 1), :]
            total = jnp.zeros((8, frames), jnp.float32)
            for c in range(0, vocab, CHUNK):
                lifted = jnp.exp(lt[c : c + CHUNK, :] - peak)
                lt[c : c + CHUNK, :] = lifted
                total = total + (lifted[:8, :] + lifted[8:, :])
            total = jnp.sum(total, axis=0, keepdims=True)
            log_total = peak + jnp.log(total)
            scale = occ_s[u : u + 1, :] / total
            blank_weight = jnp.exp(blank_s[u : u + 1, :] + (blank_logit - log_total))
            label_weight = jnp.exp(label_s[u : u + 1, :] + (label_logit - log_total))
            for c in range(0, vocab, CHUNK):
                grad_ref[c : c + CHUNK, here] = (lt[c : c + CHUNK, :] * scale).astype(jnp.bfloat16)
            for first in (0, pl.multiple_of((label // CHUNK) * CHUNK, CHUNK)):
                value = lt[pl.ds(first, CHUNK), :] * scale
                value = value - jnp.where(place + first == 0, blank_weight, 0.0)
                value = value - jnp.where(place + first == label, label_weight, 0.0)
                grad_ref[pl.ds(first, CHUNK), here] = value.astype(jnp.bfloat16)

    def accumulate(g, count):
        here = slice(g * cells, (g + count) * cells)
        term = lax.dot_general(
            act_ref[:, here],
            grad_ref[:, here],
            (((1,), (1,)), ((), ())),
            preferred_element_type=jnp.float32,
        )
        acc[...] = term if g == 0 else acc[...] + term

    activate(0)
    score_logits(0)
    for g in range(groups):
        if g + 1 < groups:
            activate(g + 1)
            score_logits(g + 1)
        differentiate(g)
        if g % 2 == 1:
            accumulate(g - 1, 2)

    if not split:
        out_refs[0][...] = acc[: width + 8, :]
        return
    parts = tm_size * label_size
    rows = width // parts
    for s in range(parts):
        label = reverse_bits(s // tm_size, label_size) ^ mine
        tm = reverse_bits(s % tm_size, tm_size) ^ row
        start = pl.multiple_of((tm * label_size + label) * rows, rows)
        to = (s % (parts // 2)) * rows
        out_refs[s // (parts // 2)][to : to + rows, :] = acc[pl.ds(start, rows), :]
    for ref in out_refs:
        ref[width // 2 :, :] = acc[width : width + 8, :]


def lane_swap(value, distance):
    lane = lax.broadcasted_iota(jnp.int32, value.shape, 1)
    return jnp.take_along_axis(value, lane ^ distance, axis=1)


def merge(low, high, distance):
    clear = (lax.broadcasted_iota(jnp.int32, low.shape, 1) & distance) == 0
    return jnp.where(clear, low, high) + lane_swap(jnp.where(clear, high, low), distance)


def backward_kernel(act_ref, grad_ref, w_ref, *rest, tm_size, label_size, columns):
    (enc_keep, enc_send, pred_keep, pred_send), (enc_acc, sums, pieces) = rest[:4], rest[4:]
    width, _ = w_ref.shape
    frames = enc_acc.shape[1]
    cells = GROUP * frames
    groups = columns // GROUP
    for g in range(groups):
        back = jnp.dot(
            w_ref[...], grad_ref[:, g * cells : (g + 1) * cells], preferred_element_type=jnp.float32
        )
        for c in range(0, width, CHUNK):
            act = act_ref[c : c + CHUNK, g * cells : (g + 1) * cells].astype(jnp.float32)
            cell = back[c : c + CHUNK, :] * (1.0 - act * act)
            parts = [cell[:, j * frames : (j + 1) * frames] for j in range(GROUP)]
            total = (parts[0] + parts[1]) + (parts[2] + parts[3])
            enc_acc[c : c + CHUNK, :] = total if g == 0 else enc_acc[c : c + CHUNK, :] + total
            pairs = [merge(parts[0], parts[2], 64), merge(parts[1], parts[3], 64)]
            folded = merge(pairs[0], pairs[1], 32)
            high = folded.astype(jnp.bfloat16)
            low = (folded - high.astype(jnp.float32)).astype(jnp.bfloat16)
            pieces[c : c + CHUNK, 2 * g * LANES : (2 * g + 1) * LANES] = high
            pieces[c : c + CHUNK, (2 * g + 1) * LANES : (2 * g + 2) * LANES] = low

    depth = 2 * groups * LANES
    place = lax.broadcasted_iota(jnp.int32, (depth, LANES), 0)
    lane = lax.broadcasted_iota(jnp.int32, (depth, LANES), 1)
    segment = (place % LANES) // (LANES // GROUP)
    column = sum(
        jnp.where(place // (2 * LANES) == g, reverse_bits(g, groups), 0) for g in range(groups)
    )
    chosen = jnp.where(column + groups * segment == lane, 1.0, 0.0).astype(jnp.bfloat16)
    sums[...] = jnp.dot(pieces[...], chosen, preferred_element_type=jnp.float32)

    mine, row = lax.axis_index("label"), lax.axis_index("tm")
    enc_width, pred_width = enc_keep.shape[2], pred_keep.shape[2]
    for s in range(label_size):
        start = pl.multiple_of((reverse_bits(s, label_size) ^ mine) * enc_width, enc_width)
        ref = (enc_keep, enc_send)[s // (label_size // 2)]
        ref[s % (label_size // 2)] = enc_acc[pl.ds(start, enc_width), :].T
    for s in range(tm_size):
        start = pl.multiple_of((reverse_bits(s, tm_size) ^ row) * pred_width, pred_width)
        ref = (pred_keep, pred_send)[s // (tm_size // 2)]
        ref[s % (tm_size // 2)] = sums[pl.ds(start, pred_width), :].T[:columns, :]


def halve(keep, send, axis):
    for bit in bits_of(lax.axis_size(axis)):
        if send is None:
            half = keep.shape[0] // 2
            keep, send = keep[:half], keep[half:]
        keep, send = keep + swap(send, axis, bit), None
    return keep


def lattice(
    encoder_out,
    predictor_out,
    label_ids,
    log_alpha,
    log_beta,
    frame_count,
    label_count,
    joint_weight,
    joint_bias,
):
    frames, columns = encoder_out.shape[1], label_ids.shape[1]
    width, vocab = joint_weight.shape
    tm_size, label_size = lax.axis_size("tm"), lax.axis_size("label")
    parts = tm_size * label_size
    rows = width // parts
    split = rows % 8 == 0
    row, mine = lax.axis_index("tm"), lax.axis_index("label")
    alpha, beta = log_alpha[0].T, log_beta[0].T
    enc_width, pred_width = encoder_out.shape[2], predictor_out.shape[2]
    f32, bf16 = jnp.float32, jnp.bfloat16
    shape = jax.ShapeDtypeStruct

    packed = enc_width == frames
    payload = encoder_out[0]
    if packed:
        payload = call(
            pack_encoder, [shape((frames + 16, enc_width), bf16)], (payload, beta), loads=2
        )[0]
    encs = gather_slots(payload, "label")
    sides = encs if packed else gather_slots(beta[0:1, :], "label")
    part, alpha, beta, weight, weight_t, bias_t, label_ids = call(
        prepare,
        [
            shape((columns + 8, pred_width), f32),
            shape(alpha.shape, f32),
            shape(beta.shape, f32),
            shape((width, vocab), bf16),
            shape((vocab, width), bf16),
            shape((vocab, frames), f32),
            shape(label_ids.shape, label_ids.dtype),
        ],
        (predictor_out[0], beta, alpha, joint_weight, joint_bias[None, :], label_ids),
        loads=6,
    )
    payload = call(
        functools.partial(pack_predictor, packed=packed),
        [shape((columns + 8, pred_width), f32)],
        (part, *sides),
    )[0]
    preds = gather_slots(payload, "tm")

    cells = columns * frames
    count, part_rows = (2, width // 2 + 8) if split else (1, width + 8)
    operands = [label_ids, frame_count, label_count, alpha, beta, weight_t, bias_t, *encs, *preds]
    act, grad, *weight_parts = call(
        functools.partial(
            forward_kernel, tm_size=tm_size, label_size=label_size, packed=packed, split=split
        ),
        [shape((width + 16, cells), bf16), shape((vocab, cells), bf16)]
        + [shape((part_rows, vocab), f32)] * count,
        operands + ([] if packed else sides),
        [pltpu.VMEM((width, frames), f32), pltpu.VMEM((width, LANES), f32)]
        + [pltpu.VMEM((columns, frames), f32)] * 3
        + [pltpu.VMEM((width + 16, vocab), f32)]
        + [pltpu.VMEM((vocab, frames), f32)] * (2 * GROUP),
        scalars=3,
        limit=FORWARD_LIMIT,
        flops=4 * width * vocab * cells,
    )
    if split:
        keep, send = weight_parts
        keep, bias_sum = keep[: width // 2], keep[width // 2 :]
    else:
        total, bias_sum = weight_parts[0][:width], weight_parts[0][width:]
        slots = total.reshape(tm_size, label_size, rows, vocab)
        for axis, size, index in ((0, tm_size, row), (1, label_size, mine)):
            order = jnp.array([reverse_bits(s, size) for s in range(size)], jnp.int32) ^ index
            slots = jnp.take(slots, order, axis=axis)
        slots = jnp.swapaxes(slots, 0, 1).reshape(width, vocab)
        keep, send = slots[: width // 2], slots[width // 2 :]
        send = jnp.concatenate([send, bias_sum], axis=0)

    stages = [("label", bit) for bit in bits_of(label_size)] + [("tm", bit) for bit in bits_of(tm_size)]
    arrived = swap(send, *stages[0])
    enc_half = shape((label_size // 2, frames, enc_width), f32)
    pred_half = shape((tm_size // 2, columns, pred_width), f32)
    enc_keep, enc_send, pred_keep, pred_send = call(
        functools.partial(backward_kernel, tm_size=tm_size, label_size=label_size, columns=columns),
        [enc_half, enc_half, pred_half, pred_half],
        (act, grad, weight),
        [
            pltpu.VMEM((width, frames), f32),
            pltpu.VMEM((width, LANES), f32),
            pltpu.VMEM((width, 2 * (columns // GROUP) * LANES), bf16),
        ],
        limit=BACKWARD_LIMIT,
        flops=2 * width * vocab * cells,
    )
    for i, _ in enumerate(stages):
        count = keep.shape[0]
        keep, bias_sum = keep + arrived[:count], bias_sum + arrived[count:]
        if i + 1 < len(stages):
            half = count // 2
            send = jnp.concatenate([keep[half:], bias_sum], axis=0)
            keep = keep[:half]
            arrived = swap(send, *stages[i + 1])
    final = jnp.concatenate([keep, bias_sum], axis=0)
    for bit in bits_of(lax.axis_size("dp")):
        final = final + swap(final, "dp", bit)
    weight_gradient = final[:rows]
    bias_rows = vocab // parts
    position = row * label_size + mine
    bias_gradient = lax.dynamic_slice_in_dim(final[rows], position * bias_rows, bias_rows, 0)

    encoder_gradient = halve(enc_keep, enc_send, "label")
    predictor_gradient = halve(pred_keep, pred_send, "tm")
    return (encoder_gradient, predictor_gradient, weight_gradient, bias_gradient)


FORWARD_LIMIT = 32
BACKWARD_LIMIT = 32


def solution(mesh):
    return jax.shard_map(
        lattice,
        mesh=mesh,
        in_specs=(
            P("dp", "tm", "label"),
            P("dp", "label", "tm"),
            P("dp", "label"),
            P("dp", "tm", "label"),
            P("dp", "tm", "label"),
            P("dp"),
            P("dp"),
            P(),
            P(),
        ),
        out_specs=(
            P("dp", "tm", "label"),
            P("dp", "label", "tm"),
            P(("tm", "label"), None),
            P(("tm", "label")),
        ),
        check_vma=False,
    )
```

```python
import functools

import jax
import jax.numpy as jnp
from jax import lax
from jax.experimental import pallas as pl
from jax.experimental.pallas import tpu as pltpu
from jax.sharding import PartitionSpec as P

GROUP = 4
CHUNK = 16
LANES = 128
FAR = -1e30
MIB = 1 << 20


def bits_of(size):
    return [1 << i for i in range(size.bit_length() - 1)]


def reverse_bits(value, size):
    width = size.bit_length() - 1
    result = 0
    for i in range(width):
        result = result | (((value >> i) & 1) << (width - 1 - i))
    return result


def swap(value, axis, bit):
    return lax.ppermute(value, axis, [(i, i ^ bit) for i in range(lax.axis_size(axis))])


def gather_slots(value, axis):
    return [value] + [swap(value, axis, s) for s in range(1, lax.axis_size(axis))]


def vmem():
    return pl.BlockSpec(memory_space=pltpu.VMEM)


def loaded(kernel, loads, outputs):
    def body(*refs):
        sources, others, outs = refs[:loads], refs[loads:-loads - 1 - outputs], refs[-loads - 1 - outputs : -loads - 1]
        targets, done = refs[-loads - 1 : -1], refs[-1]
        copies = [
            pltpu.make_async_copy(source, target, done.at[i])
            for i, (source, target) in enumerate(zip(sources, targets))
        ]
        for copy in copies:
            copy.start()
        for copy in copies:
            copy.wait()
        kernel(*targets, *others, *outs)

    return body


def call(kernel, out_shape, operands, scratch=(), scalars=0, loads=0, limit=16, flops=0):
    resident = len(operands) - scalars - loads
    scratch = list(scratch)
    operands = list(operands)
    for i in range(scalars, scalars + loads):
        operands[i] = pltpu.with_memory_space_constraint(operands[i], pltpu.HBM)
    if loads:
        kernel = loaded(kernel, loads, len(out_shape))
        scratch += [pltpu.VMEM(x.shape, x.dtype) for x in operands[scalars : scalars + loads]]
        scratch.append(pltpu.SemaphoreType.DMA((loads,)))
    return pl.pallas_call(
        kernel,
        grid_spec=pltpu.PrefetchScalarGridSpec(
            num_scalar_prefetch=scalars,
            grid=(1,),
            in_specs=[pl.BlockSpec(memory_space=pltpu.HBM)] * loads + [vmem()] * resident,
            out_specs=[vmem()] * len(out_shape),
            scratch_shapes=scratch,
        ),
        out_shape=out_shape,
        compiler_params=pltpu.CompilerParams(vmem_limit_bytes=limit * MIB),
        cost_estimate=pl.CostEstimate(flops=flops, bytes_accessed=0, transcendentals=0) if flops else None,
    )(*operands)


def pack_encoder(enc_ref, beta_ref, out_ref):
    frames = enc_ref.shape[0]
    first = beta_ref[0:1, :]
    high = first.astype(jnp.bfloat16).astype(jnp.float32)
    middle = (first - high).astype(jnp.bfloat16).astype(jnp.float32)
    low = first - high - middle
    pieces = jnp.concatenate([high, middle, low, jnp.zeros((13, frames), jnp.float32)], axis=0)
    out_ref[:frames, :] = enc_ref[...]
    out_ref[frames:, :] = pieces.astype(jnp.bfloat16)


def side_line(ref, packed):
    if not packed:
        return ref[0:1, :]
    pieces = ref[ref.shape[0] - 16 :, :].astype(jnp.float32)
    return pieces[0:1, :] + pieces[1:2, :] + pieces[2:3, :]


def pick(refs, index, packed):
    return sum(jnp.where(index == s, side_line(ref, packed), 0.0) for s, ref in enumerate(refs))


def prepare(
    pred_ref,
    beta_ref,
    alpha_ref,
    w_ref,
    bias_ref,
    ids_ref,
    limits_ref,
    pred_out,
    alpha_out,
    beta_out,
    w_out,
    wt_out,
    bias_t,
    ids_out,
    limits_out,
):
    ids_out[...] = ids_ref[...]
    limits_out[...] = limits_ref[...]
    columns = pred_ref.shape[0]
    pred_out[:columns, :] = pred_ref[...].astype(jnp.float32)
    pred_out[columns:, :] = jnp.zeros((8, pred_out.shape[1]), jnp.float32)
    pred_out[columns : columns + 1, :columns] = beta_ref[...].T[0:1, :]
    alpha_out[...] = alpha_ref[...]
    beta_out[...] = beta_ref[...]
    w_out[...] = w_ref[...]
    wt_out[...] = w_ref[...].T
    bias_t[...] = jnp.broadcast_to(bias_ref[...], (bias_t.shape[1], bias_t.shape[0])).T


def pack_predictor(pred_ref, *rest, packed):
    side_refs, out_ref = rest[:-1], rest[-1]
    columns = pred_ref.shape[0] - 8
    out_ref[...] = pred_ref[...]
    score = pick(side_refs, lax.axis_index("label"), packed)[0:1, 0:1]
    out_ref[columns + 1 : columns + 2, :] = jnp.broadcast_to(score, (1, out_ref.shape[1]))


def forward_kernel(*refs, tm_size, label_size, packed, split):
    refs = iter(refs)
    take = lambda count: [next(refs) for _ in range(count)]
    ids_ref, limits_ref, alpha_ref, beta_ref, wt_ref, bias_t = take(6)
    enc_refs, pred_refs = take(label_size), take(tm_size)
    side_refs = enc_refs if packed else take(label_size)
    act_ref, grad_ref = take(2)
    out_refs = take(2 if split else 1)
    enc_t, pred_t, occ_s, blank_s, label_s, acc = take(6)
    lts = list(refs)
    columns, frames = alpha_ref.shape
    vocab, width = wt_ref.shape
    mine, row = lax.axis_index("label"), lax.axis_index("tm")

    enc_width, pred_width = enc_refs[0].shape[1], pred_refs[0].shape[1]
    for s, ref in enumerate(enc_refs):
        start = pl.multiple_of((mine ^ s) * enc_width, enc_width)
        enc_t[pl.ds(start, enc_width), :] = ref[:frames, :].astype(jnp.float32).T
    for s, ref in enumerate(pred_refs):
        start = pl.multiple_of((row ^ s) * pred_width, pred_width)
        pred_t[pl.ds(start, pred_width), :columns] = ref[:columns, :].T

    alpha, beta = alpha_ref[...], beta_ref[...]
    score, below = 0.0, 0.0
    after = row ^ jnp.minimum(row + 1, tm_size - 1)
    for s, ref in enumerate(pred_refs):
        score = score + jnp.where(row == s, ref[columns + 1 : columns + 2, 0:1], 0.0)
        below = below + jnp.where(after == s, ref[columns : columns + 1, :columns], 0.0)
    beside = pick(side_refs, mine ^ jnp.minimum(mine + 1, label_size - 1), packed)
    diagonal = lax.broadcasted_iota(jnp.int32, (columns, columns), 0) == lax.broadcasted_iota(
        jnp.int32, (columns, columns), 1
    )
    below = jnp.sum(jnp.where(diagonal, below, 0.0), axis=1, keepdims=True)
    lane = lax.broadcasted_iota(jnp.int32, (columns, frames), 1)
    line = lax.broadcasted_iota(jnp.int32, (columns, frames), 0)
    down = jnp.where(lane == frames - 1, below, pltpu.roll(beta, frames - 1, 1))
    right = jnp.where(line == columns - 1, beside, pltpu.roll(beta, columns - 1, 0))
    frame, column = row * frames + lane, mine * columns + line
    frame_limit, label_limit = limits_ref[0:1, 0:1], limits_ref[1:2, 0:1]
    inside = (frame < frame_limit) & (column <= label_limit)
    more = frame + 1 < frame_limit
    occ_s[...] = jnp.where(inside, jnp.exp(alpha + beta - score), 0.0)
    blank_s[...] = jnp.where(
        inside & (more | (column == label_limit)),
        alpha + jnp.where(more, down, 0.0) - score,
        FAR,
    )
    label_s[...] = jnp.where(inside & (column < label_limit), alpha + right - score, FAR)

    act_ref[width:, :] = jnp.ones((act_ref.shape[0] - width, columns * frames), jnp.bfloat16)
    groups = columns // GROUP
    cells = GROUP * frames
    peaks = {}

    def column_of(g, j):
        return reverse_bits(g, groups) + groups * j

    def activate(g):
        for j in range(GROUP):
            u, at = column_of(g, j), (g * GROUP + j) * frames
            for c in range(0, width, 64):
                total = enc_t[c : c + 64, :] + pred_t[c : c + 64, u : u + 1]
                act_ref[c : c + 64, at : at + frames] = jnp.tanh(total).astype(jnp.bfloat16)

    def score_logits(g):
        product = jnp.dot(
            wt_ref[...],
            act_ref[:width, g * cells : (g + 1) * cells],
            preferred_element_type=jnp.float32,
        )
        for j in range(GROUP):
            lt = lts[(g % 2) * GROUP + j]
            logits = product[:, j * frames : (j + 1) * frames] + bias_t[...]
            lt[...] = logits
            peaks[g, j] = jnp.max(logits, axis=0, keepdims=True)

    place = lax.broadcasted_iota(jnp.int32, (CHUNK, frames), 0)

    def differentiate(g):
        for j in range(GROUP):
            u, at = column_of(g, j), (g * GROUP + j) * frames
            lt, peak = lts[(g % 2) * GROUP + j], peaks[g, j]
            here = slice(at, at + frames)
            label = ids_ref[0, u]
            blank_logit, label_logit = lt[0:1, :], lt[pl.ds(label, 1), :]
            total = jnp.zeros((8, frames), jnp.float32)
            for c in range(0, vocab, CHUNK):
                lifted = jnp.exp(lt[c : c + CHUNK, :] - peak)
                lt[c : c + CHUNK, :] = lifted
                total = total + (lifted[:8, :] + lifted[8:, :])
            total = jnp.sum(total, axis=0, keepdims=True)
            log_total = peak + jnp.log(total)
            scale = occ_s[u : u + 1, :] / total
            blank_weight = jnp.exp(blank_s[u : u + 1, :] + (blank_logit - log_total))
            label_weight = jnp.exp(label_s[u : u + 1, :] + (label_logit - log_total))
            for c in range(0, vocab, CHUNK):
                grad_ref[c : c + CHUNK, here] = (lt[c : c + CHUNK, :] * scale).astype(jnp.bfloat16)
            for first in (0, pl.multiple_of((label // CHUNK) * CHUNK, CHUNK)):
                value = lt[pl.ds(first, CHUNK), :] * scale
                value = value - jnp.where(place + first == 0, blank_weight, 0.0)
                value = value - jnp.where(place + first == label, label_weight, 0.0)
                grad_ref[pl.ds(first, CHUNK), here] = value.astype(jnp.bfloat16)

    def accumulate(g, count):
        here = slice(g * cells, (g + count) * cells)
        term = lax.dot_general(
            act_ref[:, here],
            grad_ref[:, here],
            (((1,), (1,)), ((), ())),
            preferred_element_type=jnp.float32,
        )
        acc[...] = term if g == 0 else acc[...] + term

    activate(0)
    score_logits(0)
    activate(1)
    for g in range(groups):
        if g > 0:
            accumulate(g - 1, 1)
        if g + 2 < groups:
            activate(g + 2)
        if g + 1 < groups:
            score_logits(g + 1)
        differentiate(g)
    accumulate(groups - 1, 1)

    if not split:
        out_refs[0][...] = acc[: width + 8, :]
        return
    parts, tiles = tm_size * label_size, vocab // LANES
    rows = width // parts
    for s in range(parts):
        label = reverse_bits(s // tm_size, label_size) ^ mine
        tm = reverse_bits(s % tm_size, tm_size) ^ row
        start = pl.multiple_of((tm * label_size + label) * rows, rows)
        to = (s % (parts // 2)) * rows * tiles
        for k in range(tiles):
            block = acc[pl.ds(start, rows), k * LANES : (k + 1) * LANES]
            out_refs[s // (parts // 2)][to + k * rows : to + (k + 1) * rows, :] = block
    for ref in out_refs:
        ref[width * tiles // 2 :, :] = jnp.zeros((8, LANES), jnp.float32)
        for k in range(tiles):
            at = width * tiles // 2 + k
            ref[at : at + 1, :] = acc[width : width + 1, k * LANES : (k + 1) * LANES]


def lane_swap(value, distance):
    lane = lax.broadcasted_iota(jnp.int32, value.shape, 1)
    return jnp.take_along_axis(value, lane ^ distance, axis=1)


def merge(low, high, distance):
    clear = (lax.broadcasted_iota(jnp.int32, low.shape, 1) & distance) == 0
    return jnp.where(clear, low, high) + lane_swap(jnp.where(clear, high, low), distance)


def backward_kernel(act_ref, grad_ref, w_ref, *rest, tm_size, label_size, columns):
    (enc_keep, enc_send, pred_keep, pred_send), (enc_acc, sums, pieces) = rest[:4], rest[4:]
    width, _ = w_ref.shape
    frames = enc_acc.shape[1]
    cells = GROUP * frames
    groups = columns // GROUP
    for g in range(groups):
        back = jnp.dot(
            w_ref[...], grad_ref[:, g * cells : (g + 1) * cells], preferred_element_type=jnp.float32
        )
        for c in range(0, width, CHUNK):
            act = act_ref[c : c + CHUNK, g * cells : (g + 1) * cells].astype(jnp.float32)
            cell = back[c : c + CHUNK, :] * (1.0 - act * act)
            parts = [cell[:, j * frames : (j + 1) * frames] for j in range(GROUP)]
            total = (parts[0] + parts[1]) + (parts[2] + parts[3])
            enc_acc[c : c + CHUNK, :] = total if g == 0 else enc_acc[c : c + CHUNK, :] + total
            pairs = [merge(parts[0], parts[2], 64), merge(parts[1], parts[3], 64)]
            folded = merge(pairs[0], pairs[1], 32)
            high = folded.astype(jnp.bfloat16)
            low = (folded - high.astype(jnp.float32)).astype(jnp.bfloat16)
            pieces[c : c + CHUNK, 2 * g * LANES : (2 * g + 1) * LANES] = high
            pieces[c : c + CHUNK, (2 * g + 1) * LANES : (2 * g + 2) * LANES] = low

    depth = 2 * groups * LANES
    place = lax.broadcasted_iota(jnp.int32, (depth, LANES), 0)
    lane = lax.broadcasted_iota(jnp.int32, (depth, LANES), 1)
    segment = (place % LANES) // (LANES // GROUP)
    column = sum(
        jnp.where(place // (2 * LANES) == g, reverse_bits(g, groups), 0) for g in range(groups)
    )
    chosen = jnp.where(column + groups * segment == lane, 1.0, 0.0).astype(jnp.bfloat16)
    sums[...] = jnp.dot(pieces[...], chosen, preferred_element_type=jnp.float32)

    mine, row = lax.axis_index("label"), lax.axis_index("tm")
    enc_width, pred_width = enc_keep.shape[2], pred_keep.shape[2]
    for s in range(label_size):
        start = pl.multiple_of((reverse_bits(s, label_size) ^ mine) * enc_width, enc_width)
        ref = (enc_keep, enc_send)[s // (label_size // 2)]
        ref[s % (label_size // 2)] = enc_acc[pl.ds(start, enc_width), :].T
    for s in range(tm_size):
        start = pl.multiple_of((reverse_bits(s, tm_size) ^ row) * pred_width, pred_width)
        ref = (pred_keep, pred_send)[s // (tm_size // 2)]
        ref[s % (tm_size // 2)] = sums[pl.ds(start, pred_width), :].T[:columns, :]


def finish(final_ref, weight_out, bias_out, weight_s, bias_s, done, *, label_size):
    rows, vocab = weight_s.shape
    tiles, count = vocab // LANES, bias_s.shape[1]
    for k in range(tiles):
        weight_s[:, k * LANES : (k + 1) * LANES] = final_ref[k * rows : (k + 1) * rows, :]
    copy = pltpu.make_async_copy(weight_s, weight_out, done.at[0])
    copy.start()
    first = (lax.axis_index("tm") * label_size + lax.axis_index("label")) * count
    line = jnp.zeros((1, LANES), jnp.float32)
    for k in range(tiles):
        at = rows * tiles + k
        line = line + jnp.where(first // LANES == k, final_ref[at : at + 1, :], 0.0)
    line = pltpu.roll(jnp.broadcast_to(line, (8, LANES)), lax.rem(LANES - first % LANES, LANES), 1)
    bias_s[...] = line[0:1, :count]
    other = pltpu.make_async_copy(bias_s, bias_out, done.at[1])
    other.start()
    copy.wait()
    other.wait()


def add_halves(keep_ref, arrived_ref, low_ref, high_ref):
    half = low_ref.shape[0]
    low_ref[...] = keep_ref[:half] + arrived_ref[:half]
    high_ref[...] = keep_ref[-half:] + arrived_ref[-half:]


def add_out(keep_ref, arrived_ref, out_ref, total, done, *, first):
    count = total.shape[0]
    total[...] = keep_ref[...] + arrived_ref[first : first + count]
    copy = pltpu.make_async_copy(total, out_ref.at[0], done)
    copy.start()
    copy.wait()


def write_sum(keep, arrived, first):
    rows, lanes = keep.shape
    return pl.pallas_call(
        functools.partial(add_out, first=first),
        in_specs=[vmem()] * 2,
        out_specs=pl.BlockSpec(memory_space=pltpu.HBM),
        out_shape=jax.ShapeDtypeStruct((1, rows, lanes), jnp.float32),
        scratch_shapes=[pltpu.VMEM((rows, lanes), jnp.float32), pltpu.SemaphoreType.DMA(())],
        compiler_params=pltpu.CompilerParams(vmem_limit_bytes=16 * MIB),
    )(keep, arrived)


def halve(keep, send, axis, bits):
    for bit in bits:
        if send is None:
            half = keep.shape[0] // 2
            keep, send = keep[:half], keep[half:]
        keep, send = keep + swap(send, axis, bit), None
    return keep


def lattice(
    encoder_out,
    predictor_out,
    label_ids,
    log_alpha,
    log_beta,
    frame_count,
    label_count,
    joint_weight,
    joint_bias,
):
    frames, columns = encoder_out.shape[1], label_ids.shape[1]
    width, vocab = joint_weight.shape
    tm_size, label_size = lax.axis_size("tm"), lax.axis_size("label")
    parts = tm_size * label_size
    rows = width // parts
    split = rows % 8 == 0
    row, mine = lax.axis_index("tm"), lax.axis_index("label")
    alpha, beta = log_alpha[0].T, log_beta[0].T
    enc_width, pred_width = encoder_out.shape[2], predictor_out.shape[2]
    f32, bf16 = jnp.float32, jnp.bfloat16
    shape = jax.ShapeDtypeStruct

    packed = enc_width == frames
    payload = encoder_out[0]
    if packed:
        payload = call(
            pack_encoder, [shape((frames + 16, enc_width), bf16)], (payload, beta), loads=2
        )[0]
    encs = gather_slots(payload, "label")
    sides = encs if packed else gather_slots(beta[0:1, :], "label")
    part, alpha, beta, weight, weight_t, bias_t, label_ids, limits = call(
        prepare,
        [
            shape((columns + 8, pred_width), f32),
            shape(alpha.shape, f32),
            shape(beta.shape, f32),
            shape((width, vocab), bf16),
            shape((vocab, width), bf16),
            shape((vocab, frames), f32),
            shape(label_ids.shape, label_ids.dtype),
            shape((2, LANES), jnp.int32),
        ],
        (
            predictor_out[0],
            beta,
            alpha,
            joint_weight,
            joint_bias[None, :],
            label_ids,
            jnp.broadcast_to(jnp.concatenate([frame_count, label_count])[:, None], (2, LANES)),
        ),
        loads=6,
    )
    payload = call(
        functools.partial(pack_predictor, packed=packed),
        [shape((columns + 8, pred_width), f32)],
        (part, *sides),
    )[0]
    preds = gather_slots(payload, "tm")

    cells = columns * frames
    tiles = vocab // LANES
    part_shape = (width * tiles // 2 + 8, LANES) if split else (width + 8, vocab)
    operands = [label_ids, limits, alpha, beta, weight_t, bias_t, *encs, *preds]
    act, grad, *weight_parts = call(
        functools.partial(
            forward_kernel, tm_size=tm_size, label_size=label_size, packed=packed, split=split
        ),
        [shape((width + 16, cells), bf16), shape((vocab, cells), bf16)]
        + [shape(part_shape, f32)] * (2 if split else 1),
        operands + ([] if packed else sides),
        [pltpu.VMEM((width, frames), f32), pltpu.VMEM((width, LANES), f32)]
        + [pltpu.VMEM((columns, frames), f32)] * 3
        + [pltpu.VMEM((width + 16, vocab), f32)]
        + [pltpu.VMEM((vocab, frames), f32)] * (2 * GROUP),
        scalars=1,
        limit=FORWARD_LIMIT,
        flops=4 * width * vocab * cells,
    )
    half = width * tiles // 2
    if split:
        keep, send = weight_parts
        keep, bias_sum = keep[:half], keep[half:]
    else:
        slots = weight_parts[0][:width].reshape(tm_size, label_size, rows, tiles, LANES)
        for axis, size, index in ((0, tm_size, row), (1, label_size, mine)):
            order = jnp.array([reverse_bits(s, size) for s in range(size)], jnp.int32) ^ index
            slots = jnp.take(slots, order, axis=axis)
        slots = jnp.transpose(slots, (1, 0, 3, 2, 4)).reshape(width * tiles, LANES)
        bias_sum = jnp.pad(weight_parts[0][width].reshape(tiles, LANES), ((0, 8 - tiles), (0, 0)))
        keep, send = slots[:half], jnp.concatenate([slots[half:], bias_sum], axis=0)

    stages = [("label", bit) for bit in bits_of(label_size)] + [("tm", bit) for bit in bits_of(tm_size)]
    arrived = swap(send, *stages[0])
    enc_half = shape((label_size // 2, frames, enc_width), f32)
    pred_half = shape((tm_size // 2, columns, pred_width), f32)
    enc_keep, enc_send, pred_keep, pred_send = call(
        functools.partial(backward_kernel, tm_size=tm_size, label_size=label_size, columns=columns),
        [enc_half, enc_half, pred_half, pred_half],
        (act, grad, weight),
        [
            pltpu.VMEM((width, frames), f32),
            pltpu.VMEM((width, LANES), f32),
            pltpu.VMEM((width, 2 * (columns // GROUP) * LANES), bf16),
        ],
        limit=BACKWARD_LIMIT,
        flops=2 * width * vocab * cells,
    )
    joined = pred_width == LANES
    enc_stages = bits_of(label_size)
    enc_sum, enc_rest = call(
        add_halves,
        [shape((max(label_size // 4, 1), frames, enc_width), f32)] * 2,
        (enc_keep, swap(enc_send, "label", enc_stages[0])),
    )
    pred_sum, pred_rest = pred_keep, pred_send
    for i, (axis, _) in enumerate(stages):
        count = keep.shape[0]
        keep, bias_sum = keep + arrived[:count], bias_sum + arrived[count : count + 8]
        if joined and axis == "tm":
            pred_rest = None
            if i + 1 < len(stages):
                pred_sum = pred_sum + arrived[count + 8 :].reshape(pred_sum.shape)
            else:
                predictor_gradient = write_sum(pred_sum[0], arrived, count + 8)
        if i + 1 < len(stages):
            half = count // 2
            pieces = [keep[half:], bias_sum]
            if joined and stages[i + 1][0] == "tm":
                if pred_rest is None:
                    middle = pred_sum.shape[0] // 2
                    pred_sum, pred_rest = pred_sum[:middle], pred_sum[middle:]
                pieces.append(pred_rest.reshape(-1, LANES))
            keep = keep[:half]
            arrived = swap(jnp.concatenate(pieces, axis=0), *stages[i + 1])
    final = jnp.concatenate([keep, bias_sum], axis=0)
    for bit in bits_of(lax.axis_size("dp")):
        other = swap(final, "dp", bit)
        final = final + other
    for bit in enc_stages[1:-1]:
        enc_sum = enc_sum + swap(enc_rest, "label", bit)
        half = enc_sum.shape[0] // 2
        enc_sum, enc_rest = enc_sum[:half], enc_sum[half:]
    enc_rest = swap(enc_rest[0], "label", enc_stages[-1])
    encoder_gradient = write_sum(enc_sum[0], enc_rest, 0)
    if not joined:
        predictor_gradient = halve(pred_keep, pred_send, "tm", bits_of(tm_size))
    bias_rows = vocab // parts
    weight_gradient, bias_gradient = pl.pallas_call(
        functools.partial(finish, label_size=label_size),
        in_specs=[vmem()],
        out_specs=[pl.BlockSpec(memory_space=pltpu.HBM)] * 2,
        out_shape=[shape((rows, vocab), f32), shape((1, bias_rows), f32)],
        scratch_shapes=[
            pltpu.VMEM((rows, vocab), f32),
            pltpu.VMEM((1, bias_rows), f32),
            pltpu.SemaphoreType.DMA((2,)),
        ],
        compiler_params=pltpu.CompilerParams(vmem_limit_bytes=16 * MIB),
        name="finish",
    )(final)
    return (encoder_gradient, predictor_gradient, weight_gradient, bias_gradient[0])


FORWARD_LIMIT = 32
BACKWARD_LIMIT = 32


def solution(mesh):
    return jax.shard_map(
        lattice,
        mesh=mesh,
        in_specs=(
            P("dp", "tm", "label"),
            P("dp", "label", "tm"),
            P("dp", "label"),
            P("dp", "tm", "label"),
            P("dp", "tm", "label"),
            P("dp"),
            P("dp"),
            P(),
            P(),
        ),
        out_specs=(
            P("dp", "tm", "label"),
            P("dp", "label", "tm"),
            P(("tm", "label"), None),
            P(("tm", "label")),
        ),
        check_vma=False,
    )
```

```python
import functools

import jax
import jax.numpy as jnp
from jax import lax
from jax.experimental import pallas as pl
from jax.experimental.pallas import tpu as pltpu
from jax.sharding import PartitionSpec as P

GROUP = 4
CHUNK = 16
LANES = 128
FAR = -1e30
MIB = 1 << 20


def bits_of(size):
    return [1 << i for i in range(size.bit_length() - 1)]


def reverse_bits(value, size):
    width = size.bit_length() - 1
    result = 0
    for i in range(width):
        result = result | (((value >> i) & 1) << (width - 1 - i))
    return result


def swap(value, axis, bit):
    return lax.ppermute(value, axis, [(i, i ^ bit) for i in range(lax.axis_size(axis))])


def gather_slots(value, axis):
    return [value] + [swap(value, axis, s) for s in range(1, lax.axis_size(axis))]


def vmem():
    return pl.BlockSpec(memory_space=pltpu.VMEM)


def loaded(kernel, loads, outputs):
    def body(*refs):
        sources, others, outs = refs[:loads], refs[loads:-loads - 1 - outputs], refs[-loads - 1 - outputs : -loads - 1]
        targets, done = refs[-loads - 1 : -1], refs[-1]
        copies = [
            pltpu.make_async_copy(source, target, done.at[i])
            for i, (source, target) in enumerate(zip(sources, targets))
        ]
        for copy in copies:
            copy.start()
        for copy in copies:
            copy.wait()
        kernel(*targets, *others, *outs)

    return body


def call(kernel, out_shape, operands, scratch=(), scalars=0, loads=0, limit=16, flops=0):
    resident = len(operands) - scalars - loads
    scratch = list(scratch)
    operands = list(operands)
    for i in range(scalars, scalars + loads):
        operands[i] = pltpu.with_memory_space_constraint(operands[i], pltpu.HBM)
    if loads:
        kernel = loaded(kernel, loads, len(out_shape))
        scratch += [pltpu.VMEM(x.shape, x.dtype) for x in operands[scalars : scalars + loads]]
        scratch.append(pltpu.SemaphoreType.DMA((loads,)))
    return pl.pallas_call(
        kernel,
        grid_spec=pltpu.PrefetchScalarGridSpec(
            num_scalar_prefetch=scalars,
            grid=(1,),
            in_specs=[pl.BlockSpec(memory_space=pltpu.HBM)] * loads + [vmem()] * resident,
            out_specs=[vmem()] * len(out_shape),
            scratch_shapes=scratch,
        ),
        out_shape=out_shape,
        compiler_params=pltpu.CompilerParams(vmem_limit_bytes=limit * MIB),
        cost_estimate=pl.CostEstimate(flops=flops, bytes_accessed=0, transcendentals=0) if flops else None,
    )(*operands)


def pack_encoder(enc_ref, beta_ref, out_ref):
    frames = enc_ref.shape[0]
    first = beta_ref[0:1, :]
    high = first.astype(jnp.bfloat16).astype(jnp.float32)
    middle = (first - high).astype(jnp.bfloat16).astype(jnp.float32)
    low = first - high - middle
    pieces = jnp.concatenate([high, middle, low, jnp.zeros((13, frames), jnp.float32)], axis=0)
    out_ref[:frames, :] = enc_ref[...]
    out_ref[frames:, :] = pieces.astype(jnp.bfloat16)


def side_line(ref, packed):
    if not packed:
        return ref[0:1, :]
    pieces = ref[ref.shape[0] - 16 :, :].astype(jnp.float32)
    return pieces[0:1, :] + pieces[1:2, :] + pieces[2:3, :]


def pick(refs, index, packed):
    return sum(jnp.where(index == s, side_line(ref, packed), 0.0) for s, ref in enumerate(refs))


def prepare(
    pred_ref,
    beta_ref,
    alpha_ref,
    w_ref,
    bias_ref,
    ids_ref,
    pred_out,
    alpha_out,
    beta_out,
    w_out,
    wt_out,
    bias_t,
    ids_out,
):
    ids_out[...] = ids_ref[...]
    columns = pred_ref.shape[0]
    pred_out[:columns, :] = pred_ref[...].astype(jnp.float32)
    pred_out[columns:, :] = jnp.zeros((8, pred_out.shape[1]), jnp.float32)
    pred_out[columns : columns + 1, :columns] = beta_ref[...].T[0:1, :]
    alpha_out[...] = alpha_ref[...]
    beta_out[...] = beta_ref[...]
    w_out[...] = w_ref[...]
    wt_out[...] = w_ref[...].T
    bias_t[...] = jnp.broadcast_to(bias_ref[...], (bias_t.shape[1], bias_t.shape[0])).T


def pack_predictor(pred_ref, *rest, packed):
    side_refs, out_ref = rest[:-1], rest[-1]
    columns = pred_ref.shape[0] - 8
    out_ref[...] = pred_ref[...]
    score = pick(side_refs, lax.axis_index("label"), packed)[0:1, 0:1]
    out_ref[columns + 1 : columns + 2, :] = jnp.broadcast_to(score, (1, out_ref.shape[1]))


def forward_kernel(*refs, tm_size, label_size, packed, split):
    refs = iter(refs)
    take = lambda count: [next(refs) for _ in range(count)]
    ids_ref, limits_ref, alpha_ref, beta_ref, wt_ref, bias_t = take(6)
    enc_refs, pred_refs = take(label_size), take(tm_size)
    side_refs = enc_refs if packed else take(label_size)
    act_ref, grad_ref = take(2)
    out_refs = take(2 if split else 1)
    enc_t, pred_t, occ_s, blank_s, label_s, acc = take(6)
    lts = list(refs)
    columns, frames = alpha_ref.shape
    vocab, width = wt_ref.shape
    mine, row = lax.axis_index("label"), lax.axis_index("tm")

    enc_width, pred_width = enc_refs[0].shape[1], pred_refs[0].shape[1]
    for s, ref in enumerate(enc_refs):
        start = pl.multiple_of((mine ^ s) * enc_width, enc_width)
        enc_t[pl.ds(start, enc_width), :] = ref[:frames, :].astype(jnp.float32).T
    for s, ref in enumerate(pred_refs):
        start = pl.multiple_of((row ^ s) * pred_width, pred_width)
        pred_t[pl.ds(start, pred_width), :columns] = ref[:columns, :].T

    alpha, beta = alpha_ref[...], beta_ref[...]
    score, below = 0.0, 0.0
    after = row ^ jnp.minimum(row + 1, tm_size - 1)
    for s, ref in enumerate(pred_refs):
        score = score + jnp.where(row == s, ref[columns + 1 : columns + 2, 0:1], 0.0)
        below = below + jnp.where(after == s, ref[columns : columns + 1, :columns], 0.0)
    beside = pick(side_refs, mine ^ jnp.minimum(mine + 1, label_size - 1), packed)
    diagonal = lax.broadcasted_iota(jnp.int32, (columns, columns), 0) == lax.broadcasted_iota(
        jnp.int32, (columns, columns), 1
    )
    below = jnp.sum(jnp.where(diagonal, below, 0.0), axis=1, keepdims=True)
    lane = lax.broadcasted_iota(jnp.int32, (columns, frames), 1)
    line = lax.broadcasted_iota(jnp.int32, (columns, frames), 0)
    down = jnp.where(lane == frames - 1, below, pltpu.roll(beta, frames - 1, 1))
    right = jnp.where(line == columns - 1, beside, pltpu.roll(beta, columns - 1, 0))
    frame, column = row * frames + lane, mine * columns + line
    frame_limit, label_limit = limits_ref[0:1, 0:1], limits_ref[1:2, 0:1]
    inside = (frame < frame_limit) & (column <= label_limit)
    more = frame + 1 < frame_limit
    occ_s[...] = jnp.where(inside, jnp.exp(alpha + beta - score), 0.0)
    blank_s[...] = jnp.where(
        inside & (more | (column == label_limit)),
        alpha + jnp.where(more, down, 0.0) - score,
        FAR,
    )
    label_s[...] = jnp.where(inside & (column < label_limit), alpha + right - score, FAR)

    act_ref[width:, :] = jnp.ones((act_ref.shape[0] - width, columns * frames), jnp.bfloat16)
    groups = columns // GROUP
    cells = GROUP * frames
    peaks = {}

    def column_of(g, j):
        return reverse_bits(g, groups) + groups * j

    def activate(g):
        for j in range(GROUP):
            u, at = column_of(g, j), (g * GROUP + j) * frames
            for c in range(0, width, 64):
                total = enc_t[c : c + 64, :] + pred_t[c : c + 64, u : u + 1]
                act_ref[c : c + 64, at : at + frames] = jnp.tanh(total).astype(jnp.bfloat16)

    def score_logits(g):
        product = jnp.dot(
            wt_ref[...],
            act_ref[:width, g * cells : (g + 1) * cells],
            preferred_element_type=jnp.float32,
        )
        for j in range(GROUP):
            lt = lts[(g % 2) * GROUP + j]
            logits = product[:, j * frames : (j + 1) * frames] + bias_t[...]
            lt[...] = logits
            peaks[g, j] = jnp.max(logits, axis=0, keepdims=True)

    place = lax.broadcasted_iota(jnp.int32, (CHUNK, frames), 0)

    def differentiate(g):
        for j in range(GROUP):
            u, at = column_of(g, j), (g * GROUP + j) * frames
            lt, peak = lts[(g % 2) * GROUP + j], peaks[g, j]
            here = slice(at, at + frames)
            label = ids_ref[0, u]
            blank_logit, label_logit = lt[0:1, :], lt[pl.ds(label, 1), :]
            total = jnp.zeros((8, frames), jnp.float32)
            for c in range(0, vocab, CHUNK):
                lifted = jnp.exp(lt[c : c + CHUNK, :] - peak)
                lt[c : c + CHUNK, :] = lifted
                total = total + (lifted[:8, :] + lifted[8:, :])
            total = jnp.sum(total, axis=0, keepdims=True)
            log_total = peak + jnp.log(total)
            scale = occ_s[u : u + 1, :] / total
            blank_weight = jnp.exp(blank_s[u : u + 1, :] + (blank_logit - log_total))
            label_weight = jnp.exp(label_s[u : u + 1, :] + (label_logit - log_total))
            for c in range(0, vocab, CHUNK):
                grad_ref[c : c + CHUNK, here] = (lt[c : c + CHUNK, :] * scale).astype(jnp.bfloat16)
            for first in (0, pl.multiple_of((label // CHUNK) * CHUNK, CHUNK)):
                value = lt[pl.ds(first, CHUNK), :] * scale
                value = value - jnp.where(place + first == 0, blank_weight, 0.0)
                value = value - jnp.where(place + first == label, label_weight, 0.0)
                grad_ref[pl.ds(first, CHUNK), here] = value.astype(jnp.bfloat16)

    def accumulate(g, count):
        here = slice(g * cells, (g + count) * cells)
        term = lax.dot_general(
            act_ref[:, here],
            grad_ref[:, here],
            (((1,), (1,)), ((), ())),
            preferred_element_type=jnp.float32,
        )
        acc[...] = term if g == 0 else acc[...] + term

    activate(0)
    score_logits(0)
    activate(1)
    for g in range(groups):
        if g > 0:
            accumulate(g - 1, 1)
        if g + 2 < groups:
            activate(g + 2)
        if g + 1 < groups:
            score_logits(g + 1)
        differentiate(g)
    accumulate(groups - 1, 1)

    if not split:
        out_refs[0][...] = acc[: width + 8, :]
        return
    parts, tiles = tm_size * label_size, vocab // LANES
    rows = width // parts
    for s in range(parts):
        label = reverse_bits(s // tm_size, label_size) ^ mine
        tm = s % tm_size ^ row
        start = pl.multiple_of((tm * label_size + label) * rows, rows)
        to = (s % (parts // 2)) * rows * tiles
        for k in range(tiles):
            block = acc[pl.ds(start, rows), k * LANES : (k + 1) * LANES]
            out_refs[s // (parts // 2)][to + k * rows : to + (k + 1) * rows, :] = block
    for ref in out_refs:
        ref[width * tiles // 2 :, :] = jnp.zeros((8, LANES), jnp.float32)
        for k in range(tiles):
            at = width * tiles // 2 + k
            ref[at : at + 1, :] = acc[width : width + 1, k * LANES : (k + 1) * LANES]


def lane_swap(value, distance):
    lane = lax.broadcasted_iota(jnp.int32, value.shape, 1)
    return jnp.take_along_axis(value, lane ^ distance, axis=1)


def merge(low, high, distance):
    clear = (lax.broadcasted_iota(jnp.int32, low.shape, 1) & distance) == 0
    return jnp.where(clear, low, high) + lane_swap(jnp.where(clear, high, low), distance)


def backward_kernel(act_ref, grad_ref, w_ref, *rest, tm_size, label_size, columns):
    enc_keep, enc_send, pred_out, enc_acc, sums, pieces = rest
    width, _ = w_ref.shape
    frames = enc_acc.shape[1]
    cells = GROUP * frames
    groups = columns // GROUP
    for g in range(groups):
        back = jnp.dot(
            w_ref[...], grad_ref[:, g * cells : (g + 1) * cells], preferred_element_type=jnp.float32
        )
        for c in range(0, width, CHUNK):
            act = act_ref[c : c + CHUNK, g * cells : (g + 1) * cells].astype(jnp.float32)
            cell = back[c : c + CHUNK, :] * (1.0 - act * act)
            parts = [cell[:, j * frames : (j + 1) * frames] for j in range(GROUP)]
            total = (parts[0] + parts[1]) + (parts[2] + parts[3])
            enc_acc[c : c + CHUNK, :] = total if g == 0 else enc_acc[c : c + CHUNK, :] + total
            pairs = [merge(parts[0], parts[2], 64), merge(parts[1], parts[3], 64)]
            folded = merge(pairs[0], pairs[1], 32)
            high = folded.astype(jnp.bfloat16)
            low = (folded - high.astype(jnp.float32)).astype(jnp.bfloat16)
            pieces[c : c + CHUNK, 2 * g * LANES : (2 * g + 1) * LANES] = high
            pieces[c : c + CHUNK, (2 * g + 1) * LANES : (2 * g + 2) * LANES] = low

    depth = 2 * groups * LANES
    place = lax.broadcasted_iota(jnp.int32, (depth, LANES), 0)
    lane = lax.broadcasted_iota(jnp.int32, (depth, LANES), 1)
    segment = (place % LANES) // (LANES // GROUP)
    column = sum(
        jnp.where(place // (2 * LANES) == g, reverse_bits(g, groups), 0) for g in range(groups)
    )
    chosen = jnp.where(column + groups * segment == lane, 1.0, 0.0).astype(jnp.bfloat16)
    sums[...] = jnp.dot(pieces[...], chosen, preferred_element_type=jnp.float32)

    mine, row = lax.axis_index("label"), lax.axis_index("tm")
    enc_width, pred_width = enc_keep.shape[2], pred_out.shape[2]
    for s in range(label_size):
        start = pl.multiple_of((reverse_bits(s, label_size) ^ mine) * enc_width, enc_width)
        ref = (enc_keep, enc_send)[s // (label_size // 2)]
        ref[s % (label_size // 2)] = enc_acc[pl.ds(start, enc_width), :].T
    for s in range(tm_size):
        start = pl.multiple_of((s ^ row) * pred_width, pred_width)
        pred_out[s] = sums[pl.ds(start, pred_width), :].T[:columns, :]


def finish(final_ref, weight_out, bias_out, weight_s, bias_s, done, *, label_size):
    rows, vocab = weight_s.shape
    tiles, count = vocab // LANES, bias_s.shape[1]
    for k in range(tiles):
        weight_s[:, k * LANES : (k + 1) * LANES] = final_ref[k * rows : (k + 1) * rows, :]
    copy = pltpu.make_async_copy(weight_s, weight_out, done.at[0])
    copy.start()
    first = (lax.axis_index("tm") * label_size + lax.axis_index("label")) * count
    line = jnp.zeros((1, LANES), jnp.float32)
    for k in range(tiles):
        at = rows * tiles + k
        line = line + jnp.where(first // LANES == k, final_ref[at : at + 1, :], 0.0)
    line = pltpu.roll(jnp.broadcast_to(line, (8, LANES)), lax.rem(LANES - first % LANES, LANES), 1)
    bias_s[...] = line[0:1, :count]
    other = pltpu.make_async_copy(bias_s, bias_out, done.at[1])
    other.start()
    copy.wait()
    other.wait()


def add_halves(keep_ref, arrived_ref, low_ref, high_ref):
    half = low_ref.shape[0]
    low_ref[...] = keep_ref[:half] + arrived_ref[:half]
    high_ref[...] = keep_ref[-half:] + arrived_ref[-half:]


def add_out(*refs, first):
    (*sources, out_ref, total, done) = refs
    count = total.shape[0]
    total[...] = functools.reduce(
        jnp.add, [ref[at : at + count] for ref, at in zip(sources, first, strict=True)]
    )
    copy = pltpu.make_async_copy(total, out_ref.at[0], done)
    copy.start()
    copy.wait()


def write_sum(sources, first, rows):
    lanes = sources[0].shape[1]
    return pl.pallas_call(
        functools.partial(add_out, first=first),
        in_specs=[vmem()] * len(sources),
        out_specs=pl.BlockSpec(memory_space=pltpu.HBM),
        out_shape=jax.ShapeDtypeStruct((1, rows, lanes), jnp.float32),
        scratch_shapes=[pltpu.VMEM((rows, lanes), jnp.float32), pltpu.SemaphoreType.DMA(())],
        compiler_params=pltpu.CompilerParams(vmem_limit_bytes=16 * MIB),
    )(*sources)


def lattice(
    encoder_out,
    predictor_out,
    label_ids,
    log_alpha,
    log_beta,
    frame_count,
    label_count,
    joint_weight,
    joint_bias,
):
    frames, columns = encoder_out.shape[1], label_ids.shape[1]
    width, vocab = joint_weight.shape
    tm_size, label_size = lax.axis_size("tm"), lax.axis_size("label")
    parts = tm_size * label_size
    rows = width // parts
    split = rows % 8 == 0
    row, mine = lax.axis_index("tm"), lax.axis_index("label")
    alpha, beta = log_alpha[0].T, log_beta[0].T
    enc_width, pred_width = encoder_out.shape[2], predictor_out.shape[2]
    f32, bf16 = jnp.float32, jnp.bfloat16
    shape = jax.ShapeDtypeStruct

    packed = enc_width == frames
    payload = encoder_out[0]
    if packed:
        payload = call(
            pack_encoder, [shape((frames + 16, enc_width), bf16)], (payload, beta), loads=2
        )[0]
    encs = gather_slots(payload, "label")
    sides = encs if packed else gather_slots(beta[0:1, :], "label")
    part, alpha, beta, weight, weight_t, bias_t, label_ids = call(
        prepare,
        [
            shape((columns + 8, pred_width), f32),
            shape(alpha.shape, f32),
            shape(beta.shape, f32),
            shape((width, vocab), bf16),
            shape((vocab, width), bf16),
            shape((vocab, frames), f32),
            shape(label_ids.shape, label_ids.dtype),
        ],
        (
            predictor_out[0],
            beta,
            alpha,
            joint_weight,
            joint_bias[None, :],
            label_ids,
        ),
        loads=6,
    )
    limits = jnp.concatenate([frame_count, label_count])
    limits = jnp.broadcast_to(limits[:, None], (2, LANES))
    payload = call(
        functools.partial(pack_predictor, packed=packed),
        [shape((columns + 8, pred_width), f32)],
        (part, *sides),
    )[0]
    preds = gather_slots(payload, "tm")

    cells = columns * frames
    tiles = vocab // LANES
    part_shape = (width * tiles // 2 + 8, LANES) if split else (width + 8, vocab)
    operands = [label_ids, limits, alpha, beta, weight_t, bias_t, *encs, *preds]
    act, grad, *weight_parts = call(
        functools.partial(
            forward_kernel, tm_size=tm_size, label_size=label_size, packed=packed, split=split
        ),
        [shape((width + 16, cells), bf16), shape((vocab, cells), bf16)]
        + [shape(part_shape, f32)] * (2 if split else 1),
        operands + ([] if packed else sides),
        [pltpu.VMEM((width, frames), f32), pltpu.VMEM((width, LANES), f32)]
        + [pltpu.VMEM((columns, frames), f32)] * 3
        + [pltpu.VMEM((width + 16, vocab), f32)]
        + [pltpu.VMEM((vocab, frames), f32)] * (2 * GROUP),
        scalars=1,
        limit=FORWARD_LIMIT,
        flops=4 * width * vocab * cells,
    )
    half = width * tiles // 2
    if split:
        keep, send = weight_parts
        keep, bias_sum = keep[:half], keep[half:]
    else:
        slots = weight_parts[0][:width].reshape(tm_size, label_size, rows, tiles, LANES)
        order = jnp.array([reverse_bits(s, label_size) for s in range(label_size)], jnp.int32)
        slots = jnp.take(slots, jnp.arange(tm_size) ^ row, axis=0)
        slots = jnp.take(slots, order ^ mine, axis=1)
        slots = jnp.transpose(slots, (1, 0, 3, 2, 4)).reshape(width * tiles, LANES)
        bias_sum = jnp.pad(weight_parts[0][width].reshape(tiles, LANES), ((0, 8 - tiles), (0, 0)))
        keep, send = slots[:half], jnp.concatenate([slots[half:], bias_sum], axis=0)

    label_bits = bits_of(label_size)
    arrived = swap(send, "label", label_bits[0])
    enc_half = shape((label_size // 2, frames, enc_width), f32)
    enc_keep, enc_send, pred_slots = call(
        functools.partial(backward_kernel, tm_size=tm_size, label_size=label_size, columns=columns),
        [enc_half, enc_half, shape((tm_size, columns, pred_width), f32)],
        (act, grad, weight),
        [
            pltpu.VMEM((width, frames), f32),
            pltpu.VMEM((width, LANES), f32),
            pltpu.VMEM((width, 2 * (columns // GROUP) * LANES), bf16),
        ],
        limit=BACKWARD_LIMIT,
        flops=2 * width * vocab * cells,
    )
    enc_sum, enc_rest = call(
        add_halves,
        [shape((max(label_size // 4, 1), frames, enc_width), f32)] * 2,
        (enc_keep, swap(enc_send, "label", label_bits[0])),
    )
    for bit in label_bits[1:]:
        half = keep.shape[0]
        keep, bias_sum = keep + arrived[:half], bias_sum + arrived[half:]
        half = half // 2
        arrived = swap(jnp.concatenate([keep[half:], bias_sum], axis=0), "label", bit)
        keep = keep[:half]
    for bit in label_bits[1:-1]:
        enc_sum = enc_sum + swap(enc_rest, "label", bit)
        half = enc_sum.shape[0] // 2
        enc_sum, enc_rest = enc_sum[:half], enc_sum[half:]
    enc_rest = swap(enc_rest[0], "label", label_bits[-1])
    encoder_gradient = write_sum((enc_sum[0], enc_rest), (0, 0), frames)

    half, block = keep.shape[0], rows * tiles
    keep, bias_sum = keep + arrived[:half], bias_sum + arrived[half:]
    joined = pred_width == LANES
    others, pred_others = [], []
    for s in range(1, tm_size):
        pieces = [keep[s * block : (s + 1) * block], bias_sum]
        if joined:
            pieces.append(pred_slots[s])
        others.append(swap(jnp.concatenate(pieces, axis=0), "tm", s))
        if not joined:
            pred_others.append(swap(pred_slots[s], "tm", s))
    final = jnp.concatenate([keep[:block], bias_sum], axis=0)
    final = final + functools.reduce(jnp.add, [x[: block + 8] for x in others])
    for bit in bits_of(lax.axis_size("dp")):
        other = swap(final, "dp", bit)
        final = final + other
    first = [block + 8] * len(others) if joined else [0] * len(others)
    predictor_gradient = write_sum(
        (pred_slots[0], *(others if joined else pred_others)), (0, *first), columns
    )
    bias_rows = vocab // parts
    weight_gradient, bias_gradient = pl.pallas_call(
        functools.partial(finish, label_size=label_size),
        in_specs=[vmem()],
        out_specs=[pl.BlockSpec(memory_space=pltpu.HBM)] * 2,
        out_shape=[shape((rows, vocab), f32), shape((1, bias_rows), f32)],
        scratch_shapes=[
            pltpu.VMEM((rows, vocab), f32),
            pltpu.VMEM((1, bias_rows), f32),
            pltpu.SemaphoreType.DMA((2,)),
        ],
        compiler_params=pltpu.CompilerParams(vmem_limit_bytes=16 * MIB),
        name="finish",
    )(final)
    return (encoder_gradient, predictor_gradient, weight_gradient, bias_gradient[0])


FORWARD_LIMIT = 32
BACKWARD_LIMIT = 32


def solution(mesh):
    return jax.shard_map(
        lattice,
        mesh=mesh,
        in_specs=(
            P("dp", "tm", "label"),
            P("dp", "label", "tm"),
            P("dp", "label"),
            P("dp", "tm", "label"),
            P("dp", "tm", "label"),
            P("dp"),
            P("dp"),
            P(),
            P(),
        ),
        out_specs=(
            P("dp", "tm", "label"),
            P("dp", "label", "tm"),
            P(("tm", "label"), None),
            P(("tm", "label")),
        ),
        check_vma=False,
    )
```

```python
import functools

import jax
import jax.numpy as jnp
from jax import lax
from jax.experimental import pallas as pl
from jax.experimental.pallas import tpu as pltpu
from jax.sharding import PartitionSpec as P

GROUP = 4
CHUNK = 16
LANES = 128
FAR = -1e30
MIB = 1 << 20


def bits_of(size):
    return [1 << i for i in range(size.bit_length() - 1)]


def reverse_bits(value, size):
    width = size.bit_length() - 1
    result = 0
    for i in range(width):
        result = result | (((value >> i) & 1) << (width - 1 - i))
    return result


def swap(value, axis, bit):
    return lax.ppermute(value, axis, [(i, i ^ bit) for i in range(lax.axis_size(axis))])


def gather_slots(value, axis):
    return [value] + [swap(value, axis, s) for s in range(1, lax.axis_size(axis))]


def vmem():
    return pl.BlockSpec(memory_space=pltpu.VMEM)


def loaded(kernel, loads, outputs):
    def body(*refs):
        sources, others, outs = refs[:loads], refs[loads:-loads - 1 - outputs], refs[-loads - 1 - outputs : -loads - 1]
        targets, done = refs[-loads - 1 : -1], refs[-1]
        copies = [
            pltpu.make_async_copy(source, target, done.at[i])
            for i, (source, target) in enumerate(zip(sources, targets))
        ]
        for copy in copies:
            copy.start()
        for copy in copies:
            copy.wait()
        kernel(*targets, *others, *outs)

    return body


def call(kernel, out_shape, operands, scratch=(), scalars=0, loads=0, limit=16, flops=0):
    resident = len(operands) - scalars - loads
    scratch = list(scratch)
    operands = list(operands)
    for i in range(scalars, scalars + loads):
        operands[i] = pltpu.with_memory_space_constraint(operands[i], pltpu.HBM)
    if loads:
        kernel = loaded(kernel, loads, len(out_shape))
        scratch += [pltpu.VMEM(x.shape, x.dtype) for x in operands[scalars : scalars + loads]]
        scratch.append(pltpu.SemaphoreType.DMA((loads,)))
    return pl.pallas_call(
        kernel,
        grid_spec=pltpu.PrefetchScalarGridSpec(
            num_scalar_prefetch=scalars,
            grid=(1,),
            in_specs=[pl.BlockSpec(memory_space=pltpu.HBM)] * loads + [vmem()] * resident,
            out_specs=[vmem()] * len(out_shape),
            scratch_shapes=scratch,
        ),
        out_shape=out_shape,
        compiler_params=pltpu.CompilerParams(vmem_limit_bytes=limit * MIB),
        cost_estimate=pl.CostEstimate(flops=flops, bytes_accessed=0, transcendentals=0) if flops else None,
    )(*operands)


def pack_encoder(enc_ref, beta_ref, out_ref):
    frames = enc_ref.shape[0]
    first = beta_ref[0:1, :]
    high = first.astype(jnp.bfloat16).astype(jnp.float32)
    middle = (first - high).astype(jnp.bfloat16).astype(jnp.float32)
    low = first - high - middle
    pieces = jnp.concatenate([high, middle, low, jnp.zeros((13, frames), jnp.float32)], axis=0)
    out_ref[:frames, :] = enc_ref[...]
    out_ref[frames:, :] = pieces.astype(jnp.bfloat16)


def side_line(ref, packed):
    if not packed:
        return ref[0:1, :]
    pieces = ref[ref.shape[0] - 16 :, :].astype(jnp.float32)
    return pieces[0:1, :] + pieces[1:2, :] + pieces[2:3, :]


def pick(refs, index, packed):
    return sum(jnp.where(index == s, side_line(ref, packed), 0.0) for s, ref in enumerate(refs))


def prepare(
    pred_ref,
    beta_ref,
    alpha_ref,
    w_ref,
    bias_ref,
    ids_ref,
    pred_out,
    alpha_out,
    beta_out,
    w_out,
    wt_out,
    bias_t,
    ids_out,
):
    ids_out[...] = ids_ref[...]
    columns = pred_ref.shape[0]
    pred_out[:columns, :] = pred_ref[...].astype(jnp.float32)
    pred_out[columns:, :] = jnp.zeros((8, pred_out.shape[1]), jnp.float32)
    pred_out[columns : columns + 1, :columns] = beta_ref[...].T[0:1, :]
    alpha_out[...] = alpha_ref[...]
    beta_out[...] = beta_ref[...]
    w_out[...] = w_ref[...]
    wt_out[...] = w_ref[...].T
    bias_t[...] = jnp.broadcast_to(bias_ref[...], (bias_t.shape[1], bias_t.shape[0])).T


def pack_predictor(pred_ref, *rest, packed):
    side_refs, out_ref = rest[:-1], rest[-1]
    columns = pred_ref.shape[0] - 8
    out_ref[...] = pred_ref[...]
    score = pick(side_refs, lax.axis_index("label"), packed)[0:1, 0:1]
    out_ref[columns + 1 : columns + 2, :] = jnp.broadcast_to(score, (1, out_ref.shape[1]))


def forward_kernel(*refs, tm_size, label_size, packed, split):
    refs = iter(refs)
    take = lambda count: [next(refs) for _ in range(count)]
    ids_ref, limits_ref, alpha_ref, beta_ref, wt_ref, bias_t = take(6)
    enc_refs, pred_refs = take(label_size), take(tm_size)
    side_refs = enc_refs if packed else take(label_size)
    act_ref, grad_ref = take(2)
    out_refs = take(2 if split else 1)
    enc_t, pred_t, occ_s, blank_s, label_s, acc = take(6)
    lts = list(refs)
    columns, frames = alpha_ref.shape
    vocab, width = wt_ref.shape
    mine, row = lax.axis_index("label"), lax.axis_index("tm")

    enc_width, pred_width = enc_refs[0].shape[1], pred_refs[0].shape[1]
    for s, ref in enumerate(enc_refs):
        start = pl.multiple_of((mine ^ s) * enc_width, enc_width)
        enc_t[pl.ds(start, enc_width), :] = ref[:frames, :].astype(jnp.float32).T
    for s, ref in enumerate(pred_refs):
        start = pl.multiple_of((row ^ s) * pred_width, pred_width)
        pred_t[pl.ds(start, pred_width), :columns] = ref[:columns, :].T

    alpha, beta = alpha_ref[...], beta_ref[...]
    score, below = 0.0, 0.0
    after = row ^ jnp.minimum(row + 1, tm_size - 1)
    for s, ref in enumerate(pred_refs):
        score = score + jnp.where(row == s, ref[columns + 1 : columns + 2, 0:1], 0.0)
        below = below + jnp.where(after == s, ref[columns : columns + 1, :columns], 0.0)
    beside = pick(side_refs, mine ^ jnp.minimum(mine + 1, label_size - 1), packed)
    diagonal = lax.broadcasted_iota(jnp.int32, (columns, columns), 0) == lax.broadcasted_iota(
        jnp.int32, (columns, columns), 1
    )
    below = jnp.sum(jnp.where(diagonal, below, 0.0), axis=1, keepdims=True)
    lane = lax.broadcasted_iota(jnp.int32, (columns, frames), 1)
    line = lax.broadcasted_iota(jnp.int32, (columns, frames), 0)
    down = jnp.where(lane == frames - 1, below, pltpu.roll(beta, frames - 1, 1))
    right = jnp.where(line == columns - 1, beside, pltpu.roll(beta, columns - 1, 0))
    frame, column = row * frames + lane, mine * columns + line
    frame_limit, label_limit = limits_ref[0:1, 0:1], limits_ref[1:2, 0:1]
    inside = (frame < frame_limit) & (column <= label_limit)
    more = frame + 1 < frame_limit
    occ_s[...] = jnp.where(inside, jnp.exp(alpha + beta - score), 0.0)
    blank_s[...] = jnp.where(
        inside & (more | (column == label_limit)),
        alpha + jnp.where(more, down, 0.0) - score,
        FAR,
    )
    label_s[...] = jnp.where(inside & (column < label_limit), alpha + right - score, FAR)

    act_ref[width:, :] = jnp.ones((act_ref.shape[0] - width, columns * frames), jnp.bfloat16)
    groups = columns // GROUP
    cells = GROUP * frames
    peaks = {}

    def column_of(g, j):
        return reverse_bits(g, groups) + groups * j

    def activate(g):
        for j in range(GROUP):
            u, at = column_of(g, j), (g * GROUP + j) * frames
            for c in range(0, width, 64):
                total = enc_t[c : c + 64, :] + pred_t[c : c + 64, u : u + 1]
                act_ref[c : c + 64, at : at + frames] = jnp.tanh(total).astype(jnp.bfloat16)

    def score_logits(g):
        product = jnp.dot(
            wt_ref[...],
            act_ref[:width, g * cells : (g + 1) * cells],
            preferred_element_type=jnp.float32,
        )
        for j in range(GROUP):
            lt = lts[(g % 2) * GROUP + j]
            logits = product[:, j * frames : (j + 1) * frames] + bias_t[...]
            lt[...] = logits
            peaks[g, j] = jnp.max(logits, axis=0, keepdims=True)

    place = lax.broadcasted_iota(jnp.int32, (CHUNK, frames), 0)

    def differentiate(g):
        for j in range(GROUP):
            u, at = column_of(g, j), (g * GROUP + j) * frames
            lt, peak = lts[(g % 2) * GROUP + j], peaks[g, j]
            here = slice(at, at + frames)
            label = ids_ref[0, u]
            blank_logit, label_logit = lt[0:1, :], lt[pl.ds(label, 1), :]
            total = jnp.zeros((8, frames), jnp.float32)
            for c in range(0, vocab, CHUNK):
                lifted = jnp.exp(lt[c : c + CHUNK, :] - peak)
                lt[c : c + CHUNK, :] = lifted
                total = total + (lifted[:8, :] + lifted[8:, :])
            total = jnp.sum(total, axis=0, keepdims=True)
            log_total = peak + jnp.log(total)
            scale = occ_s[u : u + 1, :] / total
            blank_weight = jnp.exp(blank_s[u : u + 1, :] + (blank_logit - log_total))
            label_weight = jnp.exp(label_s[u : u + 1, :] + (label_logit - log_total))
            for c in range(0, vocab, CHUNK):
                grad_ref[c : c + CHUNK, here] = (lt[c : c + CHUNK, :] * scale).astype(jnp.bfloat16)
            for first in (0, pl.multiple_of((label // CHUNK) * CHUNK, CHUNK)):
                value = lt[pl.ds(first, CHUNK), :] * scale
                value = value - jnp.where(place + first == 0, blank_weight, 0.0)
                value = value - jnp.where(place + first == label, label_weight, 0.0)
                grad_ref[pl.ds(first, CHUNK), here] = value.astype(jnp.bfloat16)

    def accumulate(g, count):
        here = slice(g * cells, (g + count) * cells)
        term = lax.dot_general(
            act_ref[:, here],
            grad_ref[:, here],
            (((1,), (1,)), ((), ())),
            preferred_element_type=jnp.float32,
        )
        acc[...] = term if g == 0 else acc[...] + term

    activate(0)
    score_logits(0)
    activate(1)
    for g in range(groups):
        if g > 0:
            accumulate(g - 1, 1)
        if g + 2 < groups:
            activate(g + 2)
        if g + 1 < groups:
            score_logits(g + 1)
        differentiate(g)
    accumulate(groups - 1, 1)

    if not split:
        out_refs[0][...] = acc[: width + 8, :]
        return
    parts, tiles = tm_size * label_size, vocab // LANES
    rows = width // parts
    for s in range(parts):
        label = reverse_bits(s // tm_size, label_size) ^ mine
        tm = s % tm_size ^ row
        start = pl.multiple_of((tm * label_size + label) * rows, rows)
        to = (s % (parts // 2)) * rows * tiles
        for k in range(tiles):
            block = acc[pl.ds(start, rows), k * LANES : (k + 1) * LANES]
            out_refs[s // (parts // 2)][to + k * rows : to + (k + 1) * rows, :] = block
    for ref in out_refs:
        ref[width * tiles // 2 :, :] = jnp.zeros((8, LANES), jnp.float32)
        for k in range(tiles):
            at = width * tiles // 2 + k
            ref[at : at + 1, :] = acc[width : width + 1, k * LANES : (k + 1) * LANES]


def lane_swap(value, distance):
    lane = lax.broadcasted_iota(jnp.int32, value.shape, 1)
    return jnp.take_along_axis(value, lane ^ distance, axis=1)


def merge(low, high, distance):
    clear = (lax.broadcasted_iota(jnp.int32, low.shape, 1) & distance) == 0
    return jnp.where(clear, low, high) + lane_swap(jnp.where(clear, high, low), distance)


def backward_kernel(act_ref, grad_ref, w_ref, *rest, tm_size, label_size, columns):
    enc_keep, enc_send, pred_out, enc_acc, sums, pieces = rest
    width, _ = w_ref.shape
    frames = enc_acc.shape[1]
    cells = GROUP * frames
    groups = columns // GROUP
    for g in range(groups):
        back = jnp.dot(
            w_ref[...], grad_ref[:, g * cells : (g + 1) * cells], preferred_element_type=jnp.float32
        )
        for c in range(0, width, CHUNK):
            act = act_ref[c : c + CHUNK, g * cells : (g + 1) * cells].astype(jnp.float32)
            cell = back[c : c + CHUNK, :] * (1.0 - act * act)
            parts = [cell[:, j * frames : (j + 1) * frames] for j in range(GROUP)]
            total = (parts[0] + parts[1]) + (parts[2] + parts[3])
            enc_acc[c : c + CHUNK, :] = total if g == 0 else enc_acc[c : c + CHUNK, :] + total
            pairs = [merge(parts[0], parts[2], 64), merge(parts[1], parts[3], 64)]
            folded = merge(pairs[0], pairs[1], 32)
            high = folded.astype(jnp.bfloat16)
            low = (folded - high.astype(jnp.float32)).astype(jnp.bfloat16)
            pieces[c : c + CHUNK, 2 * g * LANES : (2 * g + 1) * LANES] = high
            pieces[c : c + CHUNK, (2 * g + 1) * LANES : (2 * g + 2) * LANES] = low

    depth = 2 * groups * LANES
    place = lax.broadcasted_iota(jnp.int32, (depth, LANES), 0)
    lane = lax.broadcasted_iota(jnp.int32, (depth, LANES), 1)
    segment = (place % LANES) // (LANES // GROUP)
    column = sum(
        jnp.where(place // (2 * LANES) == g, reverse_bits(g, groups), 0) for g in range(groups)
    )
    chosen = jnp.where(column + groups * segment == lane, 1.0, 0.0).astype(jnp.bfloat16)
    sums[...] = jnp.dot(pieces[...], chosen, preferred_element_type=jnp.float32)

    mine, row = lax.axis_index("label"), lax.axis_index("tm")
    enc_width, pred_width = enc_keep.shape[2], pred_out.shape[2]
    for s in range(label_size):
        start = pl.multiple_of((reverse_bits(s, label_size) ^ mine) * enc_width, enc_width)
        ref = (enc_keep, enc_send)[s // (label_size // 2)]
        ref[s % (label_size // 2)] = enc_acc[pl.ds(start, enc_width), :].T
    for s in range(tm_size):
        start = pl.multiple_of((s ^ row) * pred_width, pred_width)
        pred_out[s] = sums[pl.ds(start, pred_width), :].T[:columns, :]


def split_kernel(keep_ref, bias_ref, arrived_ref, near_keep, far_keep, near_send, far_send):
    rows = near_keep.shape[0]
    for i, ref in enumerate((near_keep, far_keep, near_send, far_send)):
        here = slice(i * rows, (i + 1) * rows)
        ref[:rows, :] = keep_ref[here, :] + arrived_ref[here, :]
    far_send[rows:, :] = bias_ref[...] + arrived_ref[4 * rows :, :]


def block_kernel(keep_ref, bias_ref, arrived_ref, bias_more, pred_ref, *out_refs, block, first):
    bias = bias_ref[-8:, :] + bias_more[-8:, :]
    for i, ref in enumerate(out_refs):
        here = slice(i * block, (i + 1) * block)
        ref[:block, :] = keep_ref[here, :] + arrived_ref[here, :]
        ref[block : block + 8, :] = bias
        if ref.shape[0] > block + 8:
            ref[block + 8 :, :] = pred_ref[first + i]


def finish(final_ref, weight_out, bias_out, weight_s, bias_s, done, *, label_size):
    rows, vocab = weight_s.shape
    tiles, count = vocab // LANES, bias_s.shape[1]
    for k in range(tiles):
        weight_s[:, k * LANES : (k + 1) * LANES] = final_ref[k * rows : (k + 1) * rows, :]
    copy = pltpu.make_async_copy(weight_s, weight_out, done.at[0])
    copy.start()
    first = (lax.axis_index("tm") * label_size + lax.axis_index("label")) * count
    line = jnp.zeros((1, LANES), jnp.float32)
    for k in range(tiles):
        at = rows * tiles + k
        line = line + jnp.where(first // LANES == k, final_ref[at : at + 1, :], 0.0)
    line = pltpu.roll(jnp.broadcast_to(line, (8, LANES)), lax.rem(LANES - first % LANES, LANES), 1)
    bias_s[...] = line[0:1, :count]
    other = pltpu.make_async_copy(bias_s, bias_out, done.at[1])
    other.start()
    copy.wait()
    other.wait()


def add_halves(keep_ref, arrived_ref, low_ref, high_ref):
    half = low_ref.shape[0]
    low_ref[...] = keep_ref[:half] + arrived_ref[:half]
    high_ref[...] = keep_ref[-half:] + arrived_ref[-half:]


def add_out(*refs, first):
    (*sources, out_ref, total, done) = refs
    count = total.shape[0]
    total[...] = functools.reduce(
        jnp.add, [ref[at : at + count] for ref, at in zip(sources, first, strict=True)]
    )
    copy = pltpu.make_async_copy(total, out_ref.at[0], done)
    copy.start()
    copy.wait()


def write_sum(sources, first, rows):
    lanes = sources[0].shape[1]
    return pl.pallas_call(
        functools.partial(add_out, first=first),
        in_specs=[vmem()] * len(sources),
        out_specs=pl.BlockSpec(memory_space=pltpu.HBM),
        out_shape=jax.ShapeDtypeStruct((1, rows, lanes), jnp.float32),
        scratch_shapes=[pltpu.VMEM((rows, lanes), jnp.float32), pltpu.SemaphoreType.DMA(())],
        compiler_params=pltpu.CompilerParams(vmem_limit_bytes=16 * MIB),
    )(*sources)


def lattice(
    encoder_out,
    predictor_out,
    label_ids,
    log_alpha,
    log_beta,
    frame_count,
    label_count,
    joint_weight,
    joint_bias,
):
    frames, columns = encoder_out.shape[1], label_ids.shape[1]
    width, vocab = joint_weight.shape
    tm_size, label_size = lax.axis_size("tm"), lax.axis_size("label")
    parts = tm_size * label_size
    rows = width // parts
    split = rows % 8 == 0
    row, mine = lax.axis_index("tm"), lax.axis_index("label")
    alpha, beta = log_alpha[0].T, log_beta[0].T
    enc_width, pred_width = encoder_out.shape[2], predictor_out.shape[2]
    f32, bf16 = jnp.float32, jnp.bfloat16
    shape = jax.ShapeDtypeStruct

    packed = enc_width == frames
    payload = encoder_out[0]
    if packed:
        payload = call(
            pack_encoder, [shape((frames + 16, enc_width), bf16)], (payload, beta), loads=2
        )[0]
    encs = gather_slots(payload, "label")
    sides = encs if packed else gather_slots(beta[0:1, :], "label")
    part, alpha, beta, weight, weight_t, bias_t, label_ids = call(
        prepare,
        [
            shape((columns + 8, pred_width), f32),
            shape(alpha.shape, f32),
            shape(beta.shape, f32),
            shape((width, vocab), bf16),
            shape((vocab, width), bf16),
            shape((vocab, frames), f32),
            shape(label_ids.shape, label_ids.dtype),
        ],
        (
            predictor_out[0],
            beta,
            alpha,
            joint_weight,
            joint_bias[None, :],
            label_ids,
        ),
        loads=6,
    )
    limits = jnp.concatenate([frame_count, label_count])
    limits = jnp.broadcast_to(limits[:, None], (2, LANES))
    payload = call(
        functools.partial(pack_predictor, packed=packed),
        [shape((columns + 8, pred_width), f32)],
        (part, *sides),
    )[0]
    preds = gather_slots(payload, "tm")

    cells = columns * frames
    tiles = vocab // LANES
    part_shape = (width * tiles // 2 + 8, LANES) if split else (width + 8, vocab)
    operands = [label_ids, limits, alpha, beta, weight_t, bias_t, *encs, *preds]
    act, grad, *weight_parts = call(
        functools.partial(
            forward_kernel, tm_size=tm_size, label_size=label_size, packed=packed, split=split
        ),
        [shape((width + 16, cells), bf16), shape((vocab, cells), bf16)]
        + [shape(part_shape, f32)] * (2 if split else 1),
        operands + ([] if packed else sides),
        [pltpu.VMEM((width, frames), f32), pltpu.VMEM((width, LANES), f32)]
        + [pltpu.VMEM((columns, frames), f32)] * 3
        + [pltpu.VMEM((width + 16, vocab), f32)]
        + [pltpu.VMEM((vocab, frames), f32)] * (2 * GROUP),
        scalars=1,
        limit=FORWARD_LIMIT,
        flops=4 * width * vocab * cells,
    )
    half = width * tiles // 2
    if split:
        keep, send = weight_parts
        keep, bias_sum = keep[:half], keep[half:]
    else:
        slots = weight_parts[0][:width].reshape(tm_size, label_size, rows, tiles, LANES)
        order = jnp.array([reverse_bits(s, label_size) for s in range(label_size)], jnp.int32)
        slots = jnp.take(slots, jnp.arange(tm_size) ^ row, axis=0)
        slots = jnp.take(slots, order ^ mine, axis=1)
        slots = jnp.transpose(slots, (1, 0, 3, 2, 4)).reshape(width * tiles, LANES)
        bias_sum = jnp.pad(weight_parts[0][width].reshape(tiles, LANES), ((0, 8 - tiles), (0, 0)))
        keep, send = slots[:half], jnp.concatenate([slots[half:], bias_sum], axis=0)

    label_bits = bits_of(label_size)
    arrived = swap(send, "label", label_bits[0])
    enc_half = shape((label_size // 2, frames, enc_width), f32)
    enc_keep, enc_send, pred_slots = call(
        functools.partial(backward_kernel, tm_size=tm_size, label_size=label_size, columns=columns),
        [enc_half, enc_half, shape((tm_size, columns, pred_width), f32)],
        (act, grad, weight),
        [
            pltpu.VMEM((width, frames), f32),
            pltpu.VMEM((width, LANES), f32),
            pltpu.VMEM((width, 2 * (columns // GROUP) * LANES), bf16),
        ],
        limit=BACKWARD_LIMIT,
        flops=2 * width * vocab * cells,
    )
    enc_sum, enc_rest = call(
        add_halves,
        [shape((max(label_size // 4, 1), frames, enc_width), f32)] * 2,
        (enc_keep, swap(enc_send, "label", label_bits[0])),
    )
    for bit in label_bits[1:-1]:
        half = keep.shape[0]
        keep, bias_sum = keep + arrived[:half], bias_sum + arrived[half:]
        half = half // 2
        arrived = swap(jnp.concatenate([keep[half:], bias_sum], axis=0), "label", bit)
        keep = keep[:half]
    middle = keep.shape[0] // 4
    near_keep, far_keep, near_send, far_send = call(
        split_kernel,
        [shape((middle, LANES), f32)] * 3 + [shape((middle + 8, LANES), f32)],
        (keep, bias_sum, arrived),
    )
    far = swap(far_send, "label", label_bits[-1])
    near = swap(near_send, "label", label_bits[-1])
    for bit in label_bits[1:-1]:
        enc_sum = enc_sum + swap(enc_rest, "label", bit)
        half = enc_sum.shape[0] // 2
        enc_sum, enc_rest = enc_sum[:half], enc_sum[half:]
    enc_rest = swap(enc_rest[0], "label", label_bits[-1])
    encoder_gradient = write_sum((enc_sum[0], enc_rest), (0, 0), frames)

    block, joined = rows * tiles, pred_width == LANES
    payload = shape((block + 8 + columns * joined, LANES), f32)
    far_blocks = call(
        functools.partial(block_kernel, block=block, first=tm_size // 2),
        [payload] * (tm_size // 2),
        (far_keep, far_send, far, far, pred_slots),
    )
    near_blocks = call(
        functools.partial(block_kernel, block=block, first=0),
        [payload] * (tm_size // 2),
        (near_keep, far_send, near, far, pred_slots),
    )
    blocks = near_blocks + far_blocks
    others, pred_others = [], []
    for s in range(1, tm_size):
        others.append(swap(blocks[s], "tm", s))
        if not joined:
            pred_others.append(swap(pred_slots[s], "tm", s))
    final = functools.reduce(jnp.add, [x[: block + 8] for x in [blocks[0], *others]])
    for bit in bits_of(lax.axis_size("dp")):
        other = swap(final, "dp", bit)
        final = final + other
    first = [block + 8] * len(others) if joined else [0] * len(others)
    predictor_gradient = write_sum(
        (pred_slots[0], *(others if joined else pred_others)), (0, *first), columns
    )
    bias_rows = vocab // parts
    weight_gradient, bias_gradient = pl.pallas_call(
        functools.partial(finish, label_size=label_size),
        in_specs=[vmem()],
        out_specs=[pl.BlockSpec(memory_space=pltpu.HBM)] * 2,
        out_shape=[shape((rows, vocab), f32), shape((1, bias_rows), f32)],
        scratch_shapes=[
            pltpu.VMEM((rows, vocab), f32),
            pltpu.VMEM((1, bias_rows), f32),
            pltpu.SemaphoreType.DMA((2,)),
        ],
        compiler_params=pltpu.CompilerParams(vmem_limit_bytes=16 * MIB),
        name="finish",
    )(final)
    return (encoder_gradient, predictor_gradient, weight_gradient, bias_gradient[0])


FORWARD_LIMIT = 32
BACKWARD_LIMIT = 32


def solution(mesh):
    return jax.shard_map(
        lattice,
        mesh=mesh,
        in_specs=(
            P("dp", "tm", "label"),
            P("dp", "label", "tm"),
            P("dp", "label"),
            P("dp", "tm", "label"),
            P("dp", "tm", "label"),
            P("dp"),
            P("dp"),
            P(),
            P(),
        ),
        out_specs=(
            P("dp", "tm", "label"),
            P("dp", "label", "tm"),
            P(("tm", "label"), None),
            P(("tm", "label")),
        ),
        check_vma=False,
    )
```
